32 devices in a mesh: dp: 8 (over y, x, core), tensor: 4 (over z).
Axes of the slice: x: 2, y: 2, z: 4, core: 2. Of those that a mesh axis runs over, the one named last changes fastest.
Arguments:
- latents_in: bfloat16 [24576, 768], P(('dp', 'tensor')), may hold values from -6 to 6
- condition: bfloat16 [96, 768], P(('dp', 'tensor')), may hold values from -6 to 6
- ada_weight: bfloat16 [768, 4608], P(('dp', 'tensor')), may hold values from -0.21875 to 0.21875
- ada_bias: bfloat16 [4608], P(('dp', 'tensor')), may hold values from -3 to 3
- qkv_weight: bfloat16 [3, 768, 768], P(None, 'dp', 'tensor'), may hold values from -0.21875 to 0.21875
- qv_bias: bfloat16 [2, 768], P(None, 'tensor'), may hold values from -3 to 3
- proj_weight: bfloat16 [768, 768], P('tensor', 'dp'), may hold values from -0.875 to 0.875
- proj_bias: bfloat16 [768], replicated, may hold values from -3 to 3
- hidden_weight: bfloat16 [768, 3072], P('dp', 'tensor'), may hold values from -0.21875 to 0.21875
- hidden_bias: bfloat16 [3072], P('tensor'), may hold values from -3 to 3
- down_weight: bfloat16 [3072, 768], P('tensor', 'dp'), may hold values from -0.109375 to 0.109375
- down_bias: bfloat16 [768], replicated, may hold values from -3 to 3
- upstream_grad: bfloat16 [24576, 768], P(('dp', 'tensor')), may hold values from -6 to 6
Outputs:
- block_out: float32 [24576, 768], P(('dp', 'tensor'))
- input_grad: float32 [24576, 768], P(('dp', 'tensor'))
- condition_grad: float32 [96, 768], P(('dp', 'tensor'))
- ada_weight_grad: float32 [768, 4608], P(('dp', 'tensor'))
- ada_bias_grad: float32 [4608], P(('dp', 'tensor'))
- qkv_weight_grad: float32 [3, 768, 768], P(None, 'dp', 'tensor')
- qv_bias_grad: float32 [2, 768], P(None, 'tensor')
- proj_weight_grad: float32 [768, 768], P('tensor', 'dp')
- proj_bias_grad: float32 [768], replicated
- hidden_weight_grad: float32 [768, 3072], P('dp', 'tensor')
- hidden_bias_grad: float32 [3072], P('tensor')
- down_weight_grad: float32 [3072, 768], P('tensor', 'dp')
- down_bias_grad: float32 [768], replicated
The draws below stay inside these ranges and needn't reach their ends.
All inputs are finite; a program needn't handle non-finite values.
Results may differ from the reference program's by a relative error of at most 0.02.
The reference program's roundings to bfloat16 on the way count: a program that leaves them out, or rounds other values in their place, can miss the bound.
Values may be sent and summed in bfloat16 or wider, within the bound.
No kernel may reach another device: no remote copies, remote signals or barrier semaphores. Data moves between devices by JAX's collectives and lax.ppermute only.
A program may use at most 192 MiB of HBM per device.

```python
import jax
import jax.numpy as jnp
from jax import lax

D = 768
HD = 64
FF = 3072
SEQ = 256
LAT = 12
LATENTS = 96
TOKENS = 24576
N_DP = 8


def raised(entries, own_key, source, target, shards_of, factor):
    owner, partner = [(jnp.arange(entries.shape[position]) // (entries.shape[position] // shards_of)).reshape([-1 if axis == position else 1 for axis in range(entries.ndim)]) for position in (source, target)]
    chosen = jax.random.permutation(own_key, shards_of)[partner]
    strong = (owner == chosen) | (owner == (partner + shards_of // 2) % shards_of)
    return jnp.where(strong, factor * entries, entries)


def level_of(rng, shape, shards, low, high):
    factor_of, own = 1.0, jax.random.fold_in(rng, 6)
    for position, shards_of in shards:
        heights = jnp.exp(jax.random.uniform(jax.random.fold_in(own, position), (shards_of,), jnp.float32, low / len(shards), high / len(shards)))
        factor_of = factor_of * jnp.repeat(heights, shape[position] // shards_of).reshape([-1 if axis == position else 1 for axis in range(len(shape))])
    return factor_of


def noise(rng, dims, scale, most, cuts=(), held_as=jnp.bfloat16):
    entries = scale * jax.random.normal(rng, dims, jnp.float32)
    if cuts:
        entries = entries * level_of(rng, dims, cuts, -0.22, 0.18)
    return jnp.clip(entries, -most, most).astype(held_as)


def gaussian_with(rng, dims, deviation, most, cuts, heavy, kind=jnp.bfloat16):
    values = deviation * jax.random.normal(rng, dims, jnp.float32)
    if cuts:
        values = values * level_of(rng, dims, cuts, -0.22, 0.18)
    return jnp.clip(raised(values, jax.random.fold_in(rng, 3), *heavy), -most, most).astype(kind)


def setup_inputs(seed: int = 0) -> dict:
    key_of = jax.random.split(jax.random.key(seed), 14)
    latents_in = noise(key_of[0], (TOKENS, D), 1.0, 6.0, ((0, 32),))
    condition = noise(key_of[1], (LATENTS, D), 1.0, 6.0, ((0, 32),))
    ada_weight = noise(key_of[2], (D, 6 * D), D ** -0.5, 0.21875, ((0, 32),))
    ada_bias = noise(key_of[3], (6 * D,), 0.5, 3.0, ((0, 32),))
    qkv_weight = noise(key_of[4], (3, D, D), D ** -0.5, 0.21875, ((1, 8), (2, 4)))
    qv_bias = noise(key_of[5], (2, D), 0.5, 3.0, ((1, 4),))
    proj_weight = noise(key_of[6], (D, D), (D // 16) ** -0.5, 0.875, ((0, 4), (1, 8)))
    proj_bias = noise(key_of[7], (D,), 0.5, 3.0)
    hidden_weight = noise(key_of[8], (D, FF), D ** -0.5, 0.21875, ((0, 8), (1, 4)))
    hidden_bias = noise(key_of[9], (FF,), 0.5, 3.0, ((0, 4),))
    down_weight = noise(key_of[10], (FF, D), FF ** -0.5, 0.109375, ((0, 4), (1, 8)))
    down_bias = noise(key_of[11], (D,), 0.5, 3.0)
    upstream_grad = gaussian_with(key_of[12], (TOKENS, D), 1.0, 6.0, ((0, 32),), (0, 1, 32, 2.75))
    return {"latents_in": latents_in, "condition": condition, "ada_weight": ada_weight, "ada_bias": ada_bias, "qkv_weight": qkv_weight, "qv_bias": qv_bias, "proj_weight": proj_weight, "proj_bias": proj_bias, "hidden_weight": hidden_weight, "hidden_bias": hidden_bias, "down_weight": down_weight, "down_bias": down_bias, "upstream_grad": upstream_grad}


@jax.custom_vjp
def low(v):
    return lax.optimization_barrier(v.astype(jnp.bfloat16)).astype(jnp.float32)

@jax.custom_vjp
def low_back(v):
    return v

def low_keep(v):
    return (low(v), None)

def low_pass(kept, grad):
    return (grad,)

def back_keep(v):
    return (v, None)

def back_low(kept, grad):
    return (low(grad),)
low.defvjp(low_keep, low_pass)
low_back.defvjp(back_keep, back_low)

def normalize(values):
    centre = values - lax.optimization_barrier(jnp.mean(values, axis=-1, keepdims=True))
    spread = lax.optimization_barrier(jnp.mean(centre * centre, axis=-1, keepdims=True))
    return centre * lax.rsqrt(spread + 1e-06)

def block_forward(latent_rows, cond_rows, ada_weight, ada_bias, qkv_weight, qv_bias, proj_weight, proj_bias, hidden_weight, hidden_bias, down_weight, down_bias):
    highest = lax.Precision.HIGHEST
    latent_count = cond_rows.shape[0]
    head_count = D // HD
    silu_cond = low(jax.nn.silu(cond_rows))
    modulation = low_back(jnp.dot(silu_cond, ada_weight, precision=highest) + ada_bias)
    pieces = modulation.reshape(latent_count, 6, 1, D)
    shift_one, scale_one, gate_one, shift_two, scale_two, gate_two = [pieces[:, number] for number in range(6)]
    resident = latent_rows.reshape(latent_count, SEQ, D)
    input_one = low(normalize(resident) * (1.0 + scale_one) + shift_one).reshape(-1, D)
    queries = low_back(low(jnp.dot(input_one, qkv_weight[0], precision=highest) + qv_bias[0]))
    key_rows = low_back(low(jnp.dot(input_one, qkv_weight[1], precision=highest)))
    value_rows = low_back(low(jnp.dot(input_one, qkv_weight[2], precision=highest) + qv_bias[1]))

    def split_heads(matrix):
        return matrix.reshape(latent_count, SEQ, head_count, HD)
    scores = low_back(jnp.einsum('lqhd,lkhd->lhqk', split_heads(queries), split_heads(key_rows), precision=highest) * HD ** (-0.5))
    probs = jax.nn.softmax(scores, axis=-1)
    mixed = jnp.einsum('lhqk,lkhd->lqhd', low(probs), split_heads(value_rows), precision=highest).reshape(-1, D)
    mixed = low_back(low(mixed))
    attended = low_back(jnp.dot(mixed, proj_weight, precision=highest) + proj_bias).reshape(latent_count, SEQ, D)
    middle = resident + gate_one * attended
    input_two = low(normalize(middle) * (1.0 + scale_two) + shift_two).reshape(-1, D)
    preact = low_back(jnp.dot(input_two, hidden_weight, precision=highest) + hidden_bias)
    activated = low(jax.nn.gelu(preact, approximate=True))
    mlp_out = low_back(jnp.dot(activated, down_weight, precision=highest) + down_bias).reshape(latent_count, SEQ, D)
    return (middle + gate_two * mlp_out).reshape(-1, D)

def reference(latents_in, condition, ada_weight, ada_bias, qkv_weight, qv_bias, proj_weight, proj_bias, hidden_weight, hidden_bias, down_weight, down_bias, upstream_grad):
    params = (ada_weight.astype(jnp.float32), ada_bias.astype(jnp.float32), qkv_weight.astype(jnp.float32), qv_bias.astype(jnp.float32), proj_weight.astype(jnp.float32), proj_bias.astype(jnp.float32), hidden_weight.astype(jnp.float32), hidden_bias.astype(jnp.float32), down_weight.astype(jnp.float32), down_bias.astype(jnp.float32))
    latent_blocks = latents_in.astype(jnp.float32).reshape(N_DP, LAT * SEQ, D)
    cond_blocks = condition.astype(jnp.float32).reshape(N_DP, LAT, D)
    grad_blocks = upstream_grad.astype(jnp.float32).reshape(N_DP, LAT * SEQ, D)

    def step_group(totals, inputs):
        rows_in, conds_in, grads_in = inputs
        outputs, pullback = jax.vjp(block_forward, rows_in, conds_in, params[0], params[1], params[2], params[3], params[4], params[5], params[6], params[7], params[8], params[9])
        cotangents = pullback(grads_in)
        totals = jax.tree.map(lambda running, update: running + update, totals, tuple(cotangents[2:]))
        return (totals, (outputs, cotangents[0], cotangents[1]))
    zero_totals = tuple((jnp.zeros_like(param) for param in params))
    totals, (outputs, input_grads, cond_grads) = lax.scan(step_group, zero_totals, (latent_blocks, cond_blocks, grad_blocks))
    return (outputs.reshape(TOKENS, D), input_grads.reshape(TOKENS, D), cond_grads.reshape(LATENTS, D), totals[0], totals[1], totals[2], totals[3], totals[4], totals[5], totals[6], totals[7], totals[8], totals[9])
```

```python
import functools

import jax
import jax.numpy as jnp
from jax import lax
from jax.sharding import PartitionSpec as P

D = 768
HD = 64
SEQ = 256


def normalize_rows(values):
    centre = values - jnp.mean(values, axis=-1, keepdims=True)
    inverse = lax.rsqrt(jnp.mean(centre * centre, axis=-1, keepdims=True) + 1e-06)
    return (centre * inverse, inverse)


def norm_backward(grad_normed, normed, inverse):
    return inverse * (
        grad_normed
        - jnp.mean(grad_normed, axis=-1, keepdims=True)
        - normed * jnp.mean(grad_normed * normed, axis=-1, keepdims=True)
    )


def contract_rows(left, right):
    return lax.dot_general(
        left, right, (((0,), (0,)), ((), ())), preferred_element_type=jnp.float32
    )


def contract_cols(left, right):
    return lax.dot_general(
        left, right, (((1,), (1,)), ((), ())), preferred_element_type=jnp.float32
    )


def exchange(slots, axes):
    return lax.all_to_all(slots, axes, 0, 0, tiled=True)


def share(row, axes, count):
    return exchange(jnp.broadcast_to(row[None], (count,) + row.shape), axes)


def on_device(
    latents_in,
    condition,
    ada_weight,
    ada_bias,
    qkv_weight,
    qv_bias,
    proj_weight,
    proj_bias,
    hidden_weight,
    hidden_bias,
    down_weight,
    down_bias,
    upstream_grad,
    dp_size,
    tensor_size,
):
    axes = ("dp", "tensor")
    count = dp_size * tensor_size
    bf16, f32 = jnp.bfloat16, jnp.float32
    latent_count = condition.shape[0]
    local_rows = latents_in.shape[0]
    ada_rows, ada_cols = ada_weight.shape[0], ada_bias.shape[0]
    here = lax.axis_index("dp") * tensor_size + lax.axis_index("tensor")

    def gathered(shard):
        whole = lax.all_gather(shard, axes, axis=0)
        return whole.reshape((dp_size, tensor_size) + shard.shape)

    cond_float = condition.astype(f32)
    silu_value, silu_pullback = jax.vjp(jax.nn.silu, cond_float)
    silu_cond = silu_value.astype(bf16)
    sent = jnp.concatenate(
        [
            ada_weight.reshape(ada_rows, count, ada_cols).transpose(1, 0, 2).reshape(count, -1),
            silu_cond.reshape(latent_count, count, ada_rows).transpose(1, 0, 2).reshape(count, -1),
            jnp.broadcast_to(silu_cond.reshape(1, -1), (count, latent_count * D)),
        ],
        axis=1,
    )
    got = exchange(sent, axes)
    first, second = ada_rows * ada_cols, ada_rows * (ada_cols + latent_count)
    ada_columns = got[:, :first].reshape(D, ada_cols)
    silu_columns = got[:, first:second].reshape(count * latent_count, ada_rows)
    silu_all = got[:, second:].reshape(count * latent_count, D)
    modulation_columns = jnp.dot(
        silu_all, ada_columns, preferred_element_type=f32
    ) + ada_bias.astype(f32)
    modulation = exchange(modulation_columns.reshape(count, latent_count, ada_cols), axes)
    modulation = modulation.transpose(1, 0, 2)

    qkv_full = gathered(qkv_weight).transpose(2, 0, 3, 1, 4).reshape(3, D, D)
    proj_full = gathered(proj_weight).transpose(1, 2, 0, 3).reshape(D, D)
    hidden_full = gathered(hidden_weight).transpose(0, 2, 1, 3).reshape(D, -1)
    down_full = gathered(down_weight).transpose(1, 2, 0, 3).reshape(-1, D)
    qv_full = lax.all_gather(qv_bias, "tensor", axis=1, tiled=True)
    hidden_bias_full = lax.all_gather(hidden_bias, "tensor", axis=0, tiled=True)
    pieces = modulation.reshape(latent_count, 6, 1, D)
    shift_one, scale_one, gate_one, shift_two, scale_two, gate_two = [
        pieces[:, number] for number in range(6)
    ]
    resident = latents_in.astype(jnp.float32).reshape(latent_count, SEQ, D)
    normed_one, inverse_one = normalize_rows(resident)
    input_one = (
        (normed_one * (1.0 + scale_one) + shift_one).astype(jnp.bfloat16).reshape(local_rows, D)
    )
    gathered_one = input_one
    group_rows = gathered_one.shape[0]
    group_latents = group_rows // SEQ
    local_width = qkv_full.shape[2]
    head_count = local_width // HD
    scale_factor = HD ** (-0.5)
    bias_table = jnp.stack([qv_full[0], jnp.zeros_like(qv_full[0]), qv_full[1]]).astype(jnp.float32)
    projected = (
        jnp.einsum("rd,jdc->rjc", gathered_one, qkv_full, preferred_element_type=jnp.float32)
        + bias_table
    ).astype(jnp.bfloat16)

    def split_heads(matrix):
        return matrix.reshape(group_latents, SEQ, head_count, HD)

    queries = split_heads(projected[:, 0])
    key_heads = split_heads(projected[:, 1])
    value_heads = split_heads(projected[:, 2])
    scores = (
        jnp.einsum("lqhd,lkhd->lhqk", queries, key_heads, preferred_element_type=jnp.float32)
        * scale_factor
    )
    probs = jax.nn.softmax(scores, axis=-1)
    probs_low = probs.astype(jnp.bfloat16)
    mixed = (
        jnp.einsum("lhqk,lkhd->lqhd", probs_low, value_heads, preferred_element_type=jnp.float32)
        .reshape(group_rows, local_width)
        .astype(jnp.bfloat16)
    )
    attended = (
        jnp.dot(mixed, proj_full, preferred_element_type=jnp.float32)
        + proj_bias.astype(jnp.float32)
    ).reshape(latent_count, SEQ, D)
    middle = resident + gate_one * attended
    normed_two, inverse_two = normalize_rows(middle)
    input_two = (
        (normed_two * (1.0 + scale_two) + shift_two).astype(jnp.bfloat16).reshape(local_rows, D)
    )
    gathered_two = input_two
    preact = jnp.dot(
        gathered_two, hidden_full, preferred_element_type=jnp.float32
    ) + hidden_bias_full.astype(jnp.float32)
    activated, gelu_pullback = jax.vjp(lambda values: jax.nn.gelu(values, approximate=True), preact)
    activated_low = activated.astype(jnp.bfloat16)
    mlp_out = (
        jnp.dot(activated_low, down_full, preferred_element_type=jnp.float32)
        + down_bias.astype(jnp.float32)
    ).reshape(latent_count, SEQ, D)
    block_out = (middle + gate_two * mlp_out).reshape(local_rows, D)
    upstream = upstream_grad.astype(jnp.float32).reshape(latent_count, SEQ, D)
    gate_two_grad = jnp.sum(upstream * mlp_out, axis=1)
    mlp_grad = (gate_two * upstream).astype(jnp.bfloat16).reshape(local_rows, D)
    mlp_grad_all = mlp_grad
    down_bias_grad = jnp.sum(mlp_grad_all.astype(jnp.float32), axis=0)
    down_weight_grad = contract_rows(activated_low, mlp_grad_all)
    act_grad = contract_cols(mlp_grad_all, down_full)
    preact_grad = gelu_pullback(act_grad)[0].astype(jnp.bfloat16)
    hidden_bias_grad = jnp.sum(preact_grad.astype(jnp.float32), axis=0)
    hidden_weight_grad = contract_rows(gathered_two, preact_grad)
    input_two_grad = (
        contract_cols(preact_grad, hidden_full)
        .reshape(latent_count, SEQ, D)
    )
    scale_two_grad = jnp.sum(input_two_grad * normed_two, axis=1)
    shift_two_grad = jnp.sum(input_two_grad, axis=1)
    middle_grad = upstream + norm_backward(
        input_two_grad * (1.0 + scale_two), normed_two, inverse_two
    )
    gate_one_grad = jnp.sum(middle_grad * attended, axis=1)
    attended_grad = (gate_one * middle_grad).astype(jnp.bfloat16).reshape(local_rows, D)
    attended_grad_all = attended_grad
    proj_bias_grad = jnp.sum(attended_grad_all.astype(jnp.float32), axis=0)
    proj_weight_grad = contract_rows(mixed, attended_grad_all)
    mixed_grad = contract_cols(attended_grad_all, proj_full).astype(jnp.bfloat16)
    mixed_heads = split_heads(mixed_grad)
    probs_grad = jnp.einsum(
        "lqhd,lkhd->lhqk", mixed_heads, value_heads, preferred_element_type=jnp.float32
    )
    scores_grad = (
        probs * (probs_grad - jnp.sum(probs * probs_grad, axis=-1, keepdims=True))
    ).astype(jnp.bfloat16)
    query_grad = (
        jnp.einsum("lhqk,lkhd->lqhd", scores_grad, key_heads, preferred_element_type=jnp.float32)
        * scale_factor
    ).astype(jnp.bfloat16)
    key_grad = (
        jnp.einsum("lhqk,lqhd->lkhd", scores_grad, queries, preferred_element_type=jnp.float32)
        * scale_factor
    ).astype(jnp.bfloat16)
    value_grad = jnp.einsum(
        "lhqk,lqhd->lkhd", probs_low, mixed_heads, preferred_element_type=jnp.float32
    ).astype(jnp.bfloat16)
    stacked = jnp.stack(
        [
            query_grad.reshape(group_rows, local_width),
            key_grad.reshape(group_rows, local_width),
            value_grad.reshape(group_rows, local_width),
        ],
        axis=1,
    )
    qkv_weight_grad = jnp.einsum(
        "rd,rjc->jdc", gathered_one, stacked, preferred_element_type=jnp.float32
    )
    column_sums = jnp.sum(stacked.astype(jnp.float32), axis=0)
    qv_bias_grad = jnp.stack([column_sums[0], column_sums[2]])
    input_one_grad = (
        jnp.einsum("rjc,jdc->rd", stacked, qkv_full, preferred_element_type=jnp.float32)
        .reshape(latent_count, SEQ, D)
    )
    scale_one_grad = jnp.sum(input_one_grad * normed_one, axis=1)
    shift_one_grad = jnp.sum(input_one_grad, axis=1)
    input_grad = (
        middle_grad + norm_backward(input_one_grad * (1.0 + scale_one), normed_one, inverse_one)
    ).reshape(local_rows, D)
    modulation_grad = (
        jnp.stack(
            [
                shift_one_grad,
                scale_one_grad,
                gate_one_grad,
                shift_two_grad,
                scale_two_grad,
                gate_two_grad,
            ],
            axis=1,
        )
        .reshape(latent_count, 6 * D)
        .astype(jnp.bfloat16)
    )
    vectors = jnp.concatenate(
        [
            modulation_grad.reshape(-1),
            qv_bias_grad.astype(bf16).reshape(-1),
            proj_bias_grad.astype(bf16),
            hidden_bias_grad.astype(bf16),
            down_bias_grad.astype(bf16),
        ]
    )
    shared = share(vectors, axes, count)
    split = latent_count * 6 * D
    modulation_all = shared[:, :split].reshape(count * latent_count, 6 * D)
    totals = jnp.sum(shared[:, split:].astype(f32), axis=0)
    place = lax.axis_index("tensor")
    qv_bias_grad = lax.dynamic_index_in_dim(
        totals[: 2 * D].reshape(2, tensor_size, -1), place, 1, keepdims=False
    )
    proj_bias_grad = totals[2 * D : 3 * D]
    wide = hidden_bias_full.shape[0]
    hidden_bias_grad = lax.dynamic_index_in_dim(
        totals[3 * D : 3 * D + wide].reshape(tensor_size, -1), place, 0, keepdims=False
    )
    down_bias_grad = totals[3 * D + wide :]
    ada_weight_grad = contract_rows(silu_columns, modulation_all)
    ada_bias_grad = lax.dynamic_index_in_dim(
        jnp.sum(modulation_all.astype(f32), axis=0).reshape(count, ada_cols), here, 0, keepdims=False
    )
    silu_grad = exchange(
        contract_cols(modulation_all, ada_weight).reshape(count, latent_count, ada_rows), axes
    )
    condition_grad = silu_pullback(silu_grad.transpose(1, 0, 2).reshape(latent_count, D))[0]

    def scattered(blocks):
        flat = blocks.astype(bf16).reshape((-1,) + blocks.shape[-1:])
        flat = lax.psum_scatter(flat, "dp", scatter_dimension=0, tiled=True)
        return lax.psum_scatter(flat, "tensor", scatter_dimension=0, tiled=True).astype(f32)

    down_weight_grad = scattered(
        down_weight_grad.reshape(tensor_size, -1, dp_size, D // dp_size).transpose(2, 0, 1, 3)
    ).reshape(down_weight.shape)
    hidden_weight_grad = scattered(
        hidden_weight_grad.reshape(dp_size, -1, tensor_size, hidden_weight.shape[1]).transpose(0, 2, 1, 3)
    ).reshape(hidden_weight.shape)
    proj_weight_grad = scattered(
        proj_weight_grad.reshape(tensor_size, -1, dp_size, D // dp_size).transpose(2, 0, 1, 3)
    ).reshape(proj_weight.shape)
    qkv_weight_grad = scattered(
        qkv_weight_grad.reshape(3, dp_size, -1, tensor_size, D // tensor_size).transpose(1, 3, 0, 2, 4)
    ).reshape(qkv_weight.shape)
    return (
        block_out,
        input_grad,
        condition_grad,
        ada_weight_grad,
        ada_bias_grad,
        qkv_weight_grad,
        qv_bias_grad,
        proj_weight_grad,
        proj_bias_grad,
        hidden_weight_grad,
        hidden_bias_grad,
        down_weight_grad,
        down_bias_grad,
    )


def solution(mesh):
    placed = (
        P(("dp", "tensor"), None),
        P(("dp", "tensor"), None),
        P(("dp", "tensor"), None),
        P(("dp", "tensor")),
        P(None, "dp", "tensor"),
        P(None, "tensor"),
        P("tensor", "dp"),
        P(),
        P("dp", "tensor"),
        P("tensor"),
        P("tensor", "dp"),
        P(),
        P(("dp", "tensor"), None),
    )
    return jax.shard_map(
        functools.partial(
            on_device, dp_size=mesh.shape["dp"], tensor_size=mesh.shape["tensor"]
        ),
        mesh=mesh,
        in_specs=placed,
        out_specs=(
            P(("dp", "tensor"), None),
            P(("dp", "tensor"), None),
            P(("dp", "tensor"), None),
            P(("dp", "tensor"), None),
            P(("dp", "tensor")),
            P(None, "dp", "tensor"),
            P(None, "tensor"),
            P("tensor", "dp"),
            P(),
            P("dp", "tensor"),
            P("tensor"),
            P("tensor", "dp"),
            P(),
        ),
        check_vma=False,
    )
```

```python
import functools

import jax
import jax.numpy as jnp
from jax import lax
from jax.experimental import pallas as pl
from jax.experimental.pallas import tpu as pltpu
from jax.sharding import PartitionSpec as P

D = 768
HD = 64
SEQ = 256
BF16 = jnp.bfloat16
F32 = jnp.float32


def normalize_rows(values):
    centre = values - jnp.mean(values, axis=-1, keepdims=True)
    inverse = lax.rsqrt(jnp.mean(centre * centre, axis=-1, keepdims=True) + 1e-06)
    return (centre * inverse, inverse)


def norm_backward(grad_normed, normed, inverse):
    return inverse * (
        grad_normed
        - jnp.mean(grad_normed, axis=-1, keepdims=True)
        - normed * jnp.mean(grad_normed * normed, axis=-1, keepdims=True)
    )


def contract(left, right, left_axis, right_axis):
    return lax.dot_general(
        left, right, (((left_axis,), (right_axis,)), ((), ())), preferred_element_type=F32
    )


def matrix(ref, *place):
    block = ref[(slice(None),) + place]
    return block.reshape(-1, block.shape[-1])


def column_sum(values):
    return jnp.sum(values, axis=0, keepdims=True)


def head_masks(width):
    lanes = lax.broadcasted_iota(jnp.int32, (1, width), 1)
    return [
        ((lanes >= start) & (lanes < start + HD)).astype(F32).astype(BF16)
        for start in range(0, width, HD)
    ]


def head_probs(query, key):
    scores = contract(query, key, 1, 1) * HD ** (-0.5)
    raised = jnp.exp(scores - jnp.max(scores, axis=-1, keepdims=True))
    return raised * (1.0 / jnp.sum(raised, axis=-1, keepdims=True))


def attend_kernel(rows, modulation, weight, bias, input_ref, qkv_ref, mixed_ref):
    normed, _ = normalize_rows(rows[...].astype(F32))
    pieces = modulation[0]
    inputs = (normed * (1.0 + pieces[1:2]) + pieces[0:1]).astype(BF16)
    input_ref[...] = inputs
    masks = head_masks(qkv_ref.shape[-1])
    for part in range(qkv_ref.shape[0]):
        query = (contract(inputs, matrix(weight, part, 0), 1, 0) + bias[part, 0:1].astype(F32)).astype(BF16)
        key = contract(inputs, matrix(weight, part, 1), 1, 0).astype(BF16)
        value = (contract(inputs, matrix(weight, part, 2), 1, 0) + bias[part, 1:2].astype(F32)).astype(BF16)
        qkv_ref[part, 0] = query
        qkv_ref[part, 1] = key
        qkv_ref[part, 2] = value
        mixed = None
        for mask in masks:
            probs = head_probs(query * mask, key).astype(BF16)
            own = contract(probs, value * mask, 1, 0)
            mixed = own if mixed is None else mixed + own
        mixed_ref[part] = mixed.astype(BF16)


def block_kernel(
    mixed,
    rows,
    upstream_rows,
    modulation,
    proj,
    proj_bias,
    hidden,
    hidden_bias,
    down,
    down_bias,
    out_ref,
    act_ref,
    preact_grad_ref,
    mlp_grad_ref,
    input_ref,
    middle_grad_ref,
    attended_grad_ref,
    pieces_ref,
    sums_ref,
):
    parts = act_ref.shape[0]
    pieces = modulation[0]
    gate_one, shift_two, scale_two, gate_two = [pieces[k : k + 1] for k in (2, 3, 4, 5)]
    attended = proj_bias[...].astype(F32)
    for part in range(parts):
        attended = attended + contract(mixed[part], matrix(proj, part), 1, 1)
    middle = rows[...].astype(F32) + gate_one * attended
    normed, inverse = normalize_rows(middle)
    inputs = (normed * (1.0 + scale_two) + shift_two).astype(BF16)
    input_ref[...] = inputs
    upstream = upstream_rows[...].astype(F32)
    mlp_grad = (gate_two * upstream).astype(BF16)
    mlp_grad_ref[...] = mlp_grad

    @pl.when(pl.program_id(0) == 0)
    def _():
        sums_ref[...] = jnp.zeros_like(sums_ref)

    mlp = down_bias[...].astype(F32)
    input_grad = None
    root = 0.7978845608028654
    for part in range(parts):
        hidden_part = matrix(hidden, part)
        down_part = matrix(down, part)
        preact = contract(inputs, hidden_part, 1, 0) + hidden_bias[part : part + 1].astype(F32)
        square = preact * preact
        bent = jnp.tanh(root * preact * (1.0 + 0.044715 * square))
        half = 0.5 + 0.5 * bent
        activated = (preact * half).astype(BF16)
        slope = half + (0.5 * root) * preact * (1.0 - bent * bent) * (1.0 + (3 * 0.044715) * square)
        act_ref[part] = activated
        mlp = mlp + contract(activated, down_part, 1, 1)
        preact_grad = (contract(mlp_grad, down_part, 1, 0) * slope).astype(BF16)
        preact_grad_ref[part] = preact_grad
        sums_ref[part : part + 1] += column_sum(preact_grad.astype(F32))
        own = contract(preact_grad, hidden_part, 1, 1)
        input_grad = own if input_grad is None else input_grad + own
    out_ref[...] = middle + gate_two * mlp
    middle_grad = upstream + norm_backward(input_grad * (1.0 + scale_two), normed, inverse)
    middle_grad_ref[...] = middle_grad
    attended_grad = (gate_one * middle_grad).astype(BF16)
    attended_grad_ref[...] = attended_grad
    pieces_ref[0, 0:1] = column_sum(middle_grad * attended)
    pieces_ref[0, 1:2] = column_sum(input_grad)
    pieces_ref[0, 2:3] = column_sum(input_grad * normed)
    pieces_ref[0, 3:4] = column_sum(upstream * mlp)
    sums_ref[parts : parts + 1] += column_sum(attended_grad.astype(F32))
    sums_ref[parts + 1 : parts + 2] += column_sum(mlp_grad.astype(F32))


def attend_back_kernel(attended_grad, qkv, proj, grad_ref, sums_ref):
    width = qkv.shape[-1]
    masks = head_masks(width)

    @pl.when(pl.program_id(0) == 0)
    def _():
        sums_ref[...] = jnp.zeros_like(sums_ref)

    for part in range(qkv.shape[0]):
        query, key, value = qkv[part, 0], qkv[part, 1], qkv[part, 2]
        mixed_grad = contract(attended_grad[...], matrix(proj, part), 1, 0).astype(BF16)
        totals = [None, None, None]
        for mask in masks:
            own_query, own_grad = query * mask, mixed_grad * mask
            probs = head_probs(own_query, key)
            probs_grad = contract(own_grad, value, 1, 1)
            scores_grad = (
                probs * (probs_grad - jnp.sum(probs * probs_grad, axis=-1, keepdims=True))
            ).astype(BF16)
            own = (
                contract(scores_grad, key * mask, 1, 0),
                contract(scores_grad, own_query, 0, 0),
                contract(probs.astype(BF16), own_grad, 0, 0),
            )
            totals = [new if old is None else old + new for old, new in zip(totals, own)]
        for kind, factor in enumerate((HD ** (-0.5), HD ** (-0.5), 1.0)):
            low = (totals[kind] * factor).astype(BF16)
            grad_ref[part, kind] = low
            sums_ref[part, kind : kind + 1] += column_sum(low.astype(F32))


def entry_back_kernel(qkv_grad, weight, rows, modulation, middle_grad, grad_ref, pieces_ref):
    input_grad = None
    for part in range(qkv_grad.shape[0]):
        for kind in range(3):
            own = contract(qkv_grad[part, kind], matrix(weight, part, kind), 1, 1)
            input_grad = own if input_grad is None else input_grad + own
    normed, inverse = normalize_rows(rows[...].astype(F32))
    pieces = modulation[0]
    grad_ref[...] = middle_grad[...] + norm_backward(
        input_grad * (1.0 + pieces[1:2]), normed, inverse
    )
    pieces_ref[0, 0:1] = column_sum(input_grad)
    pieces_ref[0, 1:2] = column_sum(input_grad * normed)


def weight_kernel(left, right, grad_ref):
    grad = contract(left[...], right[0], 0, 0)
    grad_ref[:, 0] = grad.reshape(grad_ref.shape[0], grad_ref.shape[2], -1).astype(BF16)


def whole(array, first=0):
    return pl.BlockSpec(
        array.shape, lambda step: (0,) * array.ndim, pipeline_mode=pl.Buffered(1)
    )


def row_block(array, first=0):
    lead = array.shape[:-2]
    return pl.BlockSpec(
        lead + (SEQ, array.shape[-1]), lambda step: (0,) * len(lead) + (step + first, 0)
    )


def per_latent(array, first=0):
    return pl.BlockSpec((1,) + array.shape[1:], lambda step: (step + first, 0, 0))


def kept(array, first=0):
    return pl.BlockSpec(array.shape, lambda step: (0,) * array.ndim)


def over_latents(kernel, steps, inputs, outputs, flops, first=0, carried=()):
    shapes = [jax.ShapeDtypeStruct(shape, kind) for _, shape, kind in outputs]
    moved = sum(a.size * a.dtype.itemsize for _, a in inputs) + sum(
        s.size * s.dtype.itemsize for s in shapes
    )
    taken = len(inputs)

    def body(*refs):
        kernel(*refs[:taken], *refs[taken + len(carried) :])

    return pl.pallas_call(
        body,
        grid=(steps,),
        in_specs=[spec(array, first) for spec, array in inputs]
        + [pl.BlockSpec(memory_space=pl.ANY) for _ in carried],
        out_specs=[spec(shape, first) for (spec, _, _), shape in zip(outputs, shapes)],
        out_shape=shapes,
        input_output_aliases={taken + number: number for number in range(len(carried))},
        cost_estimate=pl.CostEstimate(flops=flops, transcendentals=0, bytes_accessed=moved),
        compiler_params=pltpu.CompilerParams(vmem_limit_bytes=56 << 20),
    )(*[array for _, array in inputs], *carried)


class Flow:
    def __init__(self, stages):
        self.stages = stages
        self.pending = next(stages)
        self.value = None

    def advance(self, results):
        try:
            self.pending = self.stages.send(results)
        except StopIteration as end:
            self.value = end.value


def settle_kernel(place, own, other, whole_ref):
    flip = place[0]
    for pair in range(own.shape[0]):
        for core, source in enumerate((own, other)):
            slot = jnp.bitwise_xor(2 * pair + core, flip)
            whole_ref[0, slot] = source[pair, 0]


def settle_heads_kernel(place, own, other, qkv_ref, proj_ref):
    flip = place[0]
    width = proj_ref.shape[-1]
    for pair in range(own.shape[0]):
        for core, source in enumerate((own, other)):
            slot = jnp.bitwise_xor(2 * pair + core, flip)
            block = source[pair, 0]
            for kind in range(3):
                qkv_ref[0, kind, slot] = block[:, kind * width : (kind + 1) * width]
            proj_ref[0, slot] = block[:, 3 * width :]


def split_rows(place, grad, keep_ref, send_ref, lanes):
    slab = keep_ref.shape[2]
    core = jnp.bitwise_and(place[0], 1)
    flip = place[0] // 2
    for pair in range(keep_ref.shape[0]):
        low = grad[2 * pair * slab : (2 * pair + 1) * slab]
        high = grad[(2 * pair + 1) * slab : (2 * pair + 2) * slab]
        slot = jnp.bitwise_xor(pair, flip)
        keep_ref[slot, 0, :, lanes] = jnp.where(core == 0, low, high)
        send_ref[slot, 0, :, lanes] = jnp.where(core == 0, high, low).astype(BF16)


def weight_split_kernel(place, left, right, keep_ref, send_ref):
    split_rows(place, contract(left[...], right[0], 0, 0), keep_ref, send_ref, slice(None))


def heads_split_kernel(place, entry, qkv_grad, outer, mixed, keep_ref, send_ref):
    width = mixed.shape[-1]
    for kind in range(3):
        grad = contract(entry[...], qkv_grad[0, kind], 0, 0)
        split_rows(place, grad, keep_ref, send_ref, slice(kind * width, (kind + 1) * width))
    grad = contract(outer[...], mixed[0], 0, 0)
    split_rows(place, grad, keep_ref, send_ref, slice(3 * width, 4 * width))


def placed_call(kernel, place, steps, inputs, outputs, flops):
    shapes = [jax.ShapeDtypeStruct(shape, kind) for _, shape, kind in outputs]
    moved = sum(a.size * a.dtype.itemsize for _, a in inputs) + sum(
        s.size * s.dtype.itemsize for s in shapes
    )
    return pl.pallas_call(
        kernel,
        grid_spec=pltpu.PrefetchScalarGridSpec(
            num_scalar_prefetch=1,
            grid=(steps,),
            in_specs=[spec(array) for spec, array in inputs],
            out_specs=[spec(shape) for (spec, _, _), shape in zip(outputs, shapes)],
        ),
        out_shape=shapes,
        cost_estimate=pl.CostEstimate(flops=flops, transcendentals=0, bytes_accessed=moved),
        compiler_params=pltpu.CompilerParams(vmem_limit_bytes=56 << 20),
    )(place, *[array for _, array in inputs])


def resident(array):
    return pl.BlockSpec(
        array.shape, lambda step, place: (0,) * array.ndim, pipeline_mode=pl.Buffered(1)
    )


def by_first(array):
    rest = (0,) * (array.ndim - 1)
    return pl.BlockSpec((1,) + array.shape[1:], lambda step, place: (step,) + rest)


def to_first(array):
    rest = (0,) * (array.ndim - 1)
    return pl.BlockSpec(
        (1,) + array.shape[1:], lambda step, place: (jnp.bitwise_xor(step, place[1]),) + rest
    )


def by_second(array):
    shape = array.shape
    return pl.BlockSpec((shape[0], 1) + shape[2:], lambda step, place: (0, step, 0, 0))


def to_second(array):
    shape = array.shape
    return pl.BlockSpec(
        (shape[0], 1) + shape[2:], lambda step, place: (0, jnp.bitwise_xor(step, place[1]), 0, 0)
    )


def weight_grad(left, right, groups=1):
    batch, tokens, width = right.shape
    shape = (groups, batch, D // groups, width)
    return pl.pallas_call(
        weight_kernel,
        grid=(batch,),
        in_specs=[whole(left), pl.BlockSpec((1, tokens, width), lambda step: (step, 0, 0))],
        out_specs=pl.BlockSpec(
            (groups, 1, D // groups, width), lambda step: (0, step, 0, 0)
        ),
        out_shape=jax.ShapeDtypeStruct(shape, BF16),
        cost_estimate=pl.CostEstimate(
            flops=2 * D * batch * tokens * width, transcendentals=0, bytes_accessed=4 * D * batch * width
        ),
        compiler_params=pltpu.CompilerParams(vmem_limit_bytes=56 << 20),
    )(left, right)


def exchange(slots, axes):
    return lax.all_to_all(slots, axes, 0, 0, tiled=True)


def on_device(
    latents_in,
    condition,
    ada_weight,
    ada_bias,
    qkv_weight,
    qv_bias,
    proj_weight,
    proj_bias,
    hidden_weight,
    hidden_bias,
    down_weight,
    down_bias,
    upstream_grad,
    dp_size,
    tensor_size,
):
    axes = ("dp", "tensor")
    count = dp_size * tensor_size
    latents = condition.shape[0]
    tokens = latents_in.shape[0]
    ada_rows, ada_cols = ada_weight.shape[0], ada_bias.shape[0]
    here = lax.axis_index("dp") * tensor_size + lax.axis_index("tensor")
    place = lax.axis_index("tensor")
    slab = D // dp_size
    direct = dp_size == 8 and tensor_size == 4 and slab % 16 == 0
    head_width, hidden_width = qkv_weight.shape[2], hidden_weight.shape[1]

    silu_value, silu_pullback = jax.vjp(jax.nn.silu, condition.astype(F32))
    silu_cond = silu_value.astype(BF16)
    sent = jnp.concatenate(
        [
            ada_weight.reshape(ada_rows, count, ada_cols).transpose(1, 0, 2).reshape(count, -1),
            silu_cond.reshape(latents, count, ada_rows).transpose(1, 0, 2).reshape(count, -1),
            jnp.broadcast_to(
                jnp.concatenate([silu_cond.reshape(-1), qv_bias.reshape(-1), hidden_bias])[None],
                (count, latents * D + 2 * head_width + hidden_width),
            ),
        ],
        axis=1,
    )
    def swap(array, mask):
        return lax.ppermute(array, axes, [(device, device ^ mask) for device in range(count)])

    def slot(flows, inputs, run):
        moving = [[array for array, _ in flow.pending] for flow in flows]
        moving, inputs = lax.optimization_barrier((moving, inputs))
        results = [
            [swap(array, mask) for array, (_, mask) in zip(arrays, flow.pending)]
            for arrays, flow in zip(moving, flows)
        ]
        results, made = lax.optimization_barrier((results, run(*inputs)))
        for flow, arrived in zip(flows, results):
            flow.advance(arrived)
        return made

    across, along, upward = [tensor_size << bit for bit in range(3)]
    half = tensor_size // 2
    position = jnp.stack([lax.axis_index("dp"), place])

    def gather_stages(shard):
        line = yield [(shard, mask) for mask in range(1, tensor_size)]
        line = jnp.stack([shard] + line)
        side, above = yield [(line, along), (line, upward)]
        first, second = yield [(side[:half], upward), (above[half:], along)]
        own = jnp.stack([line, side, above, jnp.concatenate([first, second])])
        (other,) = yield [(own, across)]
        return own, other

    def reduce_stages(keep, send):
        (arrived,) = yield [(send, across)]
        summed = keep + arrived.astype(F32)
        line, side, above, far = [summed[number] for number in range(4)]
        low = [block.astype(BF16) for block in (side[:half], above[half:], far[:half], far[half:])]
        arrived = yield list(zip(low, (along, upward, along, upward)))
        side_low, above_high, far_low, far_high = [block.astype(F32) for block in arrived]
        arrived = yield [
            ((above[:half] + far_low).astype(BF16), upward),
            ((side[half:] + far_high).astype(BF16), along),
        ]
        low = line[:half] + side_low + arrived[0].astype(F32)
        high = line[half:] + above_high + arrived[1].astype(F32)
        pieces = [low[number] for number in range(half)] + [high[number] for number in range(half)]
        arrived = yield [(pieces[mask].astype(BF16), mask) for mask in range(1, tensor_size)]
        return sum([block.astype(F32) for block in arrived], pieces[0])

    def gathered(shard):
        whole_set = lax.all_gather(shard, axes, axis=0)
        whole_set = whole_set.reshape((dp_size, tensor_size) + shard.shape)
        rows = whole_set.ndim - 2
        whole_set = jnp.moveaxis(whole_set, 0, rows - 1)
        return whole_set.reshape((1,) + whole_set.shape[: rows - 1] + (D, shard.shape[-1]))

    def scattered(blocks):
        blocks = blocks[0].reshape(-1, dp_size, slab, blocks.shape[-1]).swapaxes(0, 1)
        flat = blocks.reshape(-1, blocks.shape[-1])
        flat = lax.psum_scatter(flat, "dp", scatter_dimension=0, tiled=True)
        return lax.psum_scatter(flat, "tensor", scatter_dimension=0, tiled=True).astype(F32)

    def settled(own, other):
        shape = (tensor_size, dp_size, slab, D)
        (whole_set,) = placed_call(
            settle_kernel,
            position,
            tensor_size,
            [(by_second, own), (by_second, other)],
            [(to_first, shape, BF16)],
            0,
        )
        return whole_set.reshape(1, tensor_size, D, D)

    def settled_heads(own, other):
        qkv_set, proj_set = placed_call(
            settle_heads_kernel,
            position,
            tensor_size,
            [(by_second, own), (by_second, other)],
            [
                (to_first, (tensor_size, 3, dp_size, slab, head_width), BF16),
                (to_first, (tensor_size, dp_size, slab, head_width), BF16),
            ],
            0,
        )
        return (
            qkv_set.reshape(1, tensor_size, 3, D, head_width),
            proj_set.reshape(1, tensor_size, D, head_width),
        )

    ends = [ada_rows * ada_cols]
    for size in (ada_rows * latents, latents * D, 2 * head_width):
        ends.append(ends[-1] + size)

    def modulate(silu_all, ada_columns):
        columns = jnp.dot(silu_all, ada_columns, preferred_element_type=F32) + ada_bias.astype(F32)
        back = exchange(columns.reshape(count, latents, ada_cols), axes)
        return back.transpose(1, 0, 2).reshape(latents, 6, D)

    heads_in = hidden_in = down_in = None
    if direct:
        heads_in, hidden_in, down_in = [
            Flow(gather_stages(shard))
            for shard in (
                jnp.concatenate(list(qkv_weight) + [proj_weight.T], axis=1),
                hidden_weight,
                down_weight.T,
            )
        ]
    got = slot([heads_in] if direct else [], (sent,), lambda slots: exchange(slots, axes))
    ada_columns = got[:, : ends[0]].reshape(D, ada_cols)
    silu_columns = got[:, ends[0] : ends[1]].reshape(count * latents, ada_rows)
    silu_all = got[:, ends[1] : ends[2]].reshape(count * latents, D)
    qv_full = got[:tensor_size, ends[2] : ends[3]].reshape(tensor_size, 2, head_width)
    hidden_bias_full = got[:tensor_size, ends[3] :]
    modulation = slot(
        [heads_in, hidden_in] if direct else [], (silu_all, ada_columns), modulate
    )
    if direct:
        slot([heads_in, hidden_in, down_in], (), lambda: ())
        slot([heads_in, hidden_in, down_in], (), lambda: ())
        qkv_full, proj_full = settled_heads(*heads_in.value)
    else:
        qkv_full = gathered(qkv_weight)
        proj_full = gathered(proj_weight.T)
        hidden_full = gathered(hidden_weight)
        down_full = gathered(down_weight.T)

    def spread(*last):
        return (tensor_size,) + last

    unit = 2 * tokens * D * D

    def attend(rows, pieces, weight, bias):
        return over_latents(
            attend_kernel,
            latents,
            [(row_block, rows), (per_latent, pieces), (whole, weight), (whole, bias)],
            [
                (row_block, (tokens, D), BF16),
                (row_block, spread(3, tokens, head_width), BF16),
                (row_block, spread(tokens, head_width), BF16),
            ],
            5 * unit,
        )

    input_one, qkv, mixed = slot(
        [hidden_in, down_in] if direct else [],
        (latents_in, modulation, qkv_full, qv_full),
        attend,
    )
    if direct:
        hidden_full = slot([down_in], hidden_in.value, settled)
        down_full = settled(*down_in.value)
    (
        block_out,
        activated,
        preact_grad,
        mlp_grad,
        input_two,
        middle_grad,
        attended_grad,
        late_pieces,
        late_sums,
    ) = over_latents(
        block_kernel,
        latents,
        [
            (row_block, mixed),
            (row_block, latents_in),
            (row_block, upstream_grad),
            (per_latent, modulation),
            (whole, proj_full),
            (whole, proj_bias[None]),
            (whole, hidden_full),
            (whole, hidden_bias_full),
            (whole, down_full),
            (whole, down_bias[None]),
        ],
        [
            (row_block, (tokens, D), F32),
            (row_block, spread(tokens, hidden_width), BF16),
            (row_block, spread(tokens, hidden_width), BF16),
            (row_block, (tokens, D), BF16),
            (row_block, (tokens, D), BF16),
            (row_block, (tokens, D), F32),
            (row_block, (tokens, D), BF16),
            (per_latent, (latents, 4, D), F32),
            (kept, (tensor_size + 2, D), F32),
        ],
        18 * unit,
    )

    split_shape = (dp_size // 2, tensor_size, slab, D)
    split_out = [(to_second, split_shape, F32), (to_second, split_shape, BF16)]

    def square_grad(left, right):
        return placed_call(
            weight_split_kernel,
            position,
            tensor_size,
            [(resident, left), (by_first, right)],
            split_out,
            4 * unit,
        )

    def heads_grad(entry, heads, outer, inner):
        return placed_call(
            heads_split_kernel,
            position,
            tensor_size,
            [(resident, entry), (by_first, heads), (resident, outer), (by_first, inner)],
            split_out,
            4 * unit,
        )

    def attend_back(first, steps, carried):
        def run(outer, heads, weight, *kept_back):
            return over_latents(
                attend_back_kernel,
                steps,
                [(row_block, outer), (row_block, heads), (whole, weight)],
                [
                    (row_block, spread(3, tokens, head_width), BF16),
                    (kept, spread(3, head_width), F32),
                ],
                4 * unit * steps,
                first,
                kept_back,
            )

        return (attended_grad, qkv, proj_full) + carried, run

    def entry_back(first, steps, carried):
        def run(heads, weight, rows, pieces, outer, *kept_back):
            return over_latents(
                entry_back_kernel,
                steps,
                [
                    (row_block, heads),
                    (whole, weight),
                    (row_block, rows),
                    (per_latent, pieces),
                    (row_block, outer),
                ],
                [(row_block, (tokens, D), F32), (per_latent, (latents, 2, D), F32)],
                unit * steps,
                first,
                kept_back,
            )

        return (qkv_grad, qkv_full, latents_in, modulation, middle_grad) + carried, run

    if direct:
        down_out = Flow(reduce_stages(*square_grad(mlp_grad, activated)))
        hidden_out = Flow(
            reduce_stages(*slot([down_out], (input_two, preact_grad), square_grad))
        )
        qkv_sums, carried = 0.0, ()
        for latent in range(latents):
            flows = [flow for flow in (down_out, hidden_out) if flow.value is None]
            qkv_grad, own_sums = slot(flows, *attend_back(latent, 1, carried))
            carried, qkv_sums = (qkv_grad,), qkv_sums + own_sums
        flows = [flow for flow in (down_out, hidden_out) if flow.value is None]
        heads_out = Flow(
            reduce_stages(*slot(flows, (input_one, qkv_grad, attended_grad, mixed), heads_grad))
        )
        input_grad, early_pieces = slot([heads_out], *entry_back(0, latents, ()))
        while heads_out.value is None:
            slot([heads_out], (), lambda: ())
        while hidden_out.value is None:
            slot([hidden_out], (), lambda: ())
        down_weight_grad, hidden_weight_grad = down_out.value.T, hidden_out.value
        packed_grad = heads_out.value.reshape(slab, 4, head_width)
        qkv_weight_grad = packed_grad[:, :3].swapaxes(0, 1)
        proj_weight_grad = packed_grad[:, 3].T
    else:
        inputs, run = attend_back(0, latents, ())
        qkv_grad, qkv_sums = run(*inputs)
        down_weight_grad = scattered(weight_grad(mlp_grad, activated)).T
        hidden_weight_grad = scattered(weight_grad(input_two, preact_grad))
        proj_weight_grad = scattered(weight_grad(attended_grad, mixed)).T
        qkv_weight_grad = scattered(
            weight_grad(input_one, qkv_grad.reshape(-1, tokens, head_width))
        ).reshape(qkv_weight.shape)
        inputs, run = entry_back(0, latents, ())
        input_grad, early_pieces = run(*inputs)
    modulation_grad = jnp.concatenate([early_pieces, late_pieces], axis=1).astype(BF16)
    vectors = jnp.concatenate(
        [
            modulation_grad.reshape(-1),
            qkv_sums[:, ::2].astype(BF16).reshape(-1),
            late_sums.astype(BF16).reshape(-1),
        ]
    )
    shared = exchange(jnp.broadcast_to(vectors[None], (count, vectors.shape[0])), axes)
    split = latents * 6 * D
    modulation_all = shared[:, :split].reshape(count * latents, 6 * D)
    ones = jnp.ones((1, count), BF16)
    totals = contract(ones, shared[:, split:], 1, 0)[0]
    qv_bias_grad = lax.dynamic_index_in_dim(
        totals[: 2 * D].reshape(tensor_size, 2, head_width), place, 0, keepdims=False
    )
    rest = totals[2 * D :].reshape(tensor_size + 2, D)
    hidden_bias_grad = lax.dynamic_index_in_dim(rest, place, 0, keepdims=False)
    proj_bias_grad, down_bias_grad = rest[tensor_size], rest[tensor_size + 1]
    ada_weight_grad = contract(silu_columns, modulation_all, 0, 0)
    ada_bias_grad = lax.dynamic_index_in_dim(
        contract(jnp.ones((1, count * latents), BF16), modulation_all, 1, 0).reshape(count, ada_cols), here, 0, keepdims=False
    )
    silu_grad = exchange(
        contract(modulation_all, ada_weight, 1, 1).reshape(count, latents, ada_rows), axes
    )
    condition_grad = silu_pullback(silu_grad.transpose(1, 0, 2).reshape(latents, D))[0]
    return (
        block_out,
        input_grad,
        condition_grad,
        ada_weight_grad,
        ada_bias_grad,
        qkv_weight_grad,
        qv_bias_grad,
        proj_weight_grad,
        proj_bias_grad,
        hidden_weight_grad,
        hidden_bias_grad,
        down_weight_grad,
        down_bias_grad,
    )


def solution(mesh):
    both = ("dp", "tensor")
    placed = (
        P(both, None),
        P(both, None),
        P(both, None),
        P(both),
        P(None, "dp", "tensor"),
        P(None, "tensor"),
        P("tensor", "dp"),
        P(),
        P("dp", "tensor"),
        P("tensor"),
        P("tensor", "dp"),
        P(),
        P(both, None),
    )
    return jax.shard_map(
        functools.partial(
            on_device, dp_size=mesh.shape["dp"], tensor_size=mesh.shape["tensor"]
        ),
        mesh=mesh,
        in_specs=placed,
        out_specs=(P(both, None), P(both, None)) + placed[1:-1],
        check_vma=False,
    )
```

```python
import functools

import jax
import jax.numpy as jnp
from jax import lax
from jax.experimental import pallas as pl
from jax.experimental.pallas import tpu as pltpu
from jax.sharding import PartitionSpec as P

D = 768
HD = 64
SEQ = 256
BF16 = jnp.bfloat16
F32 = jnp.float32


def normalize_rows(values):
    centre = values - jnp.mean(values, axis=-1, keepdims=True)
    inverse = lax.rsqrt(jnp.mean(centre * centre, axis=-1, keepdims=True) + 1e-06)
    return (centre * inverse, inverse)


def norm_backward(grad_normed, normed, inverse):
    return inverse * (
        grad_normed
        - jnp.mean(grad_normed, axis=-1, keepdims=True)
        - normed * jnp.mean(grad_normed * normed, axis=-1, keepdims=True)
    )


def contract(left, right, left_axis, right_axis):
    return lax.dot_general(
        left, right, (((left_axis,), (right_axis,)), ((), ())), preferred_element_type=F32
    )


def matrix(ref, *place):
    block = ref[(slice(None),) + place]
    return block.reshape(-1, block.shape[-1])


def column_sum(values):
    return jnp.sum(values, axis=0, keepdims=True)


def head_masks(width):
    lanes = lax.broadcasted_iota(jnp.int32, (1, width), 1)
    return [
        ((lanes >= start) & (lanes < start + HD)).astype(F32).astype(BF16)
        for start in range(0, width, HD)
    ]


def head_probs(query, key):
    scores = contract(query, key, 1, 1) * HD ** (-0.5)
    raised = jnp.exp(scores - jnp.max(scores, axis=-1, keepdims=True))
    return raised * (1.0 / jnp.sum(raised, axis=-1, keepdims=True))


def attend_kernel(rows, modulation, weight, bias, input_ref, qkv_ref, mixed_ref):
    normed, _ = normalize_rows(rows[...].astype(F32))
    pieces = modulation[0]
    inputs = (normed * (1.0 + pieces[1:2]) + pieces[0:1]).astype(BF16)
    input_ref[...] = inputs
    masks = head_masks(qkv_ref.shape[-1])
    for part in range(qkv_ref.shape[0]):
        query = (contract(inputs, matrix(weight, part, 0), 1, 0) + bias[part, 0:1].astype(F32)).astype(BF16)
        key = contract(inputs, matrix(weight, part, 1), 1, 0).astype(BF16)
        value = (contract(inputs, matrix(weight, part, 2), 1, 0) + bias[part, 1:2].astype(F32)).astype(BF16)
        qkv_ref[part, 0] = query
        qkv_ref[part, 1] = key
        qkv_ref[part, 2] = value
        mixed = None
        for mask in masks:
            probs = head_probs(query * mask, key).astype(BF16)
            own = contract(probs, value * mask, 1, 0)
            mixed = own if mixed is None else mixed + own
        mixed_ref[part] = mixed.astype(BF16)


def block_kernel(
    mixed,
    rows,
    upstream_rows,
    modulation,
    proj,
    proj_bias,
    hidden,
    hidden_bias,
    down,
    down_bias,
    out_ref,
    act_ref,
    preact_grad_ref,
    mlp_grad_ref,
    input_ref,
    middle_grad_ref,
    attended_grad_ref,
    pieces_ref,
    sums_ref,
):
    parts = act_ref.shape[0]
    pieces = modulation[0]
    gate_one, shift_two, scale_two, gate_two = [pieces[k : k + 1] for k in (2, 3, 4, 5)]
    attended = proj_bias[...].astype(F32)
    for part in range(parts):
        attended = attended + contract(mixed[part], matrix(proj, part), 1, 1)
    middle = rows[...].astype(F32) + gate_one * attended
    normed, inverse = normalize_rows(middle)
    inputs = (normed * (1.0 + scale_two) + shift_two).astype(BF16)
    input_ref[...] = inputs
    upstream = upstream_rows[...].astype(F32)
    mlp_grad = (gate_two * upstream).astype(BF16)
    mlp_grad_ref[...] = mlp_grad

    @pl.when(pl.program_id(0) == 0)
    def _():
        sums_ref[...] = jnp.zeros_like(sums_ref)

    mlp = down_bias[...].astype(F32)
    input_grad = None
    root = 0.7978845608028654
    for part in range(parts):
        hidden_part = matrix(hidden, part)
        down_part = matrix(down, part)
        preact = contract(inputs, hidden_part, 1, 0) + hidden_bias[part : part + 1].astype(F32)
        square = preact * preact
        bent = jnp.tanh(root * preact * (1.0 + 0.044715 * square))
        half = 0.5 + 0.5 * bent
        activated = (preact * half).astype(BF16)
        slope = half + (0.5 * root) * preact * (1.0 - bent * bent) * (1.0 + (3 * 0.044715) * square)
        act_ref[part] = activated
        mlp = mlp + contract(activated, down_part, 1, 1)
        preact_grad = (contract(mlp_grad, down_part, 1, 0) * slope).astype(BF16)
        preact_grad_ref[part] = preact_grad
        sums_ref[part : part + 1] += column_sum(preact_grad.astype(F32))
        own = contract(preact_grad, hidden_part, 1, 1)
        input_grad = own if input_grad is None else input_grad + own
    out_ref[...] = middle + gate_two * mlp
    middle_grad = upstream + norm_backward(input_grad * (1.0 + scale_two), normed, inverse)
    middle_grad_ref[...] = middle_grad
    attended_grad = (gate_one * middle_grad).astype(BF16)
    attended_grad_ref[...] = attended_grad
    pieces_ref[0, 0:1] = column_sum(middle_grad * attended)
    pieces_ref[0, 1:2] = column_sum(input_grad)
    pieces_ref[0, 2:3] = column_sum(input_grad * normed)
    pieces_ref[0, 3:4] = column_sum(upstream * mlp)
    sums_ref[parts : parts + 1] += column_sum(attended_grad.astype(F32))
    sums_ref[parts + 1 : parts + 2] += column_sum(mlp_grad.astype(F32))


def block_settle_kernel(
    mixed,
    rows,
    upstream_rows,
    modulation,
    proj,
    proj_bias,
    hidden_own,
    hidden_other,
    hidden_bias,
    down_own,
    down_other,
    down_bias,
    place,
    *refs,
):
    made, (hidden, down) = refs[:-2], refs[-2:]

    @pl.when(pl.program_id(0) == 0)
    def _():
        for number in range(hidden.shape[1]):
            line = jnp.bitwise_xor(number, place[1])
            for pair in range(hidden_own.shape[0]):
                for core, sources in enumerate(
                    ((hidden_own, down_own), (hidden_other, down_other))
                ):
                    spot = jnp.bitwise_xor(2 * pair + core, place[0])
                    hidden[spot, line] = sources[0][pair, number]
                    down[spot, line] = sources[1][pair, number]

    block_kernel(
        mixed,
        rows,
        upstream_rows,
        modulation,
        proj,
        proj_bias,
        hidden,
        hidden_bias,
        down,
        down_bias,
        *made,
    )


def attend_back_kernel(attended_grad, qkv, proj, grad_ref, sums_ref):
    width = qkv.shape[-1]
    masks = head_masks(width)

    @pl.when(pl.program_id(0) == 0)
    def _():
        sums_ref[...] = jnp.zeros_like(sums_ref)

    for part in range(qkv.shape[0]):
        query, key, value = qkv[part, 0], qkv[part, 1], qkv[part, 2]
        mixed_grad = contract(attended_grad[...], matrix(proj, part), 1, 0).astype(BF16)
        totals = [None, None, None]
        for mask in masks:
            own_query, own_grad = query * mask, mixed_grad * mask
            probs = head_probs(own_query, key)
            probs_grad = contract(own_grad, value, 1, 1)
            scores_grad = (
                probs * (probs_grad - jnp.sum(probs * probs_grad, axis=-1, keepdims=True))
            ).astype(BF16)
            own = (
                contract(scores_grad, key * mask, 1, 0),
                contract(scores_grad, own_query, 0, 0),
                contract(probs.astype(BF16), own_grad, 0, 0),
            )
            totals = [new if old is None else old + new for old, new in zip(totals, own)]
        for kind, factor in enumerate((HD ** (-0.5), HD ** (-0.5), 1.0)):
            low = (totals[kind] * factor).astype(BF16)
            grad_ref[part, kind] = low
            sums_ref[part, kind : kind + 1] += column_sum(low.astype(F32))


def entry_back_kernel(qkv_grad, weight, rows, modulation, middle_grad, grad_ref, pieces_ref):
    input_grad = None
    for part in range(qkv_grad.shape[0]):
        for kind in range(3):
            own = contract(qkv_grad[part, kind], matrix(weight, part, kind), 1, 1)
            input_grad = own if input_grad is None else input_grad + own
    normed, inverse = normalize_rows(rows[...].astype(F32))
    pieces = modulation[0]
    grad_ref[...] = middle_grad[...] + norm_backward(
        input_grad * (1.0 + pieces[1:2]), normed, inverse
    )
    pieces_ref[0, 0:1] = column_sum(input_grad)
    pieces_ref[0, 1:2] = column_sum(input_grad * normed)


def weight_kernel(left, right, grad_ref):
    grad = contract(left[...], right[0], 0, 0)
    grad_ref[:, 0] = grad.reshape(grad_ref.shape[0], grad_ref.shape[2], -1).astype(BF16)


def whole(array, first=0):
    return pl.BlockSpec(
        array.shape, lambda step: (0,) * array.ndim, pipeline_mode=pl.Buffered(1)
    )


def row_block(array, first=0):
    lead = array.shape[:-2]
    return pl.BlockSpec(
        lead + (SEQ, array.shape[-1]), lambda step: (0,) * len(lead) + (step + first, 0)
    )


def per_latent(array, first=0):
    return pl.BlockSpec((1,) + array.shape[1:], lambda step: (step + first, 0, 0))


def scalars(array, first=0):
    return pl.BlockSpec(memory_space=pltpu.SMEM)


def kept(array, first=0):
    return pl.BlockSpec(array.shape, lambda step: (0,) * array.ndim)


def over_latents(kernel, steps, inputs, outputs, flops, first=0, carried=(), scratch=()):
    shapes = [jax.ShapeDtypeStruct(shape, kind) for _, shape, kind in outputs]
    moved = sum(a.size * a.dtype.itemsize for _, a in inputs) + sum(
        s.size * s.dtype.itemsize for s in shapes
    )
    taken = len(inputs)

    def body(*refs):
        kernel(*refs[:taken], *refs[taken + len(carried) :])

    return pl.pallas_call(
        body,
        grid=(steps,),
        in_specs=[spec(array, first) for spec, array in inputs]
        + [pl.BlockSpec(memory_space=pl.ANY) for _ in carried],
        out_specs=[spec(shape, first) for (spec, _, _), shape in zip(outputs, shapes)],
        out_shape=shapes,
        scratch_shapes=list(scratch),
        input_output_aliases={taken + number: number for number in range(len(carried))},
        cost_estimate=pl.CostEstimate(flops=flops, transcendentals=0, bytes_accessed=moved),
        compiler_params=pltpu.CompilerParams(vmem_limit_bytes=56 << 20),
    )(*[array for _, array in inputs], *carried)


class Flow:
    def __init__(self, stages):
        self.stages = stages
        self.pending = next(stages)
        self.value = None

    def advance(self, results):
        try:
            self.pending = self.stages.send(results)
        except StopIteration as end:
            self.value = end.value


def settle_heads_kernel(place, own, other, qkv_ref, proj_ref):
    flip = place[0]
    width = proj_ref.shape[-1]
    for pair in range(own.shape[0]):
        for core, source in enumerate((own, other)):
            slot = jnp.bitwise_xor(2 * pair + core, flip)
            block = source[pair, 0]
            for kind in range(3):
                qkv_ref[0, kind, slot] = block[:, kind * width : (kind + 1) * width]
            proj_ref[0, slot] = block[:, 3 * width :]


def latent_back_kernel(
    attended_grad,
    qkv,
    proj,
    weight,
    rows,
    modulation,
    middle_grad,
    heads_ref,
    grad_ref,
    pieces_ref,
    sums_ref,
):
    attend_back_kernel(attended_grad, qkv, proj, heads_ref, sums_ref)
    entry_back_kernel(heads_ref, weight, rows, modulation, middle_grad, grad_ref, pieces_ref)


def split_rows(place, grad, keep_ref, send_ref, lanes):
    slab = keep_ref.shape[2]
    core = jnp.bitwise_and(place[0], 1)
    flip = place[0] // 2
    for pair in range(keep_ref.shape[0]):
        low = grad[2 * pair * slab : (2 * pair + 1) * slab]
        high = grad[(2 * pair + 1) * slab : (2 * pair + 2) * slab]
        slot = jnp.bitwise_xor(pair, flip)
        keep_ref[slot, 0, :, lanes] = jnp.where(core == 0, low, high)
        send_ref[slot, 0, :, lanes] = jnp.where(core == 0, high, low).astype(BF16)


def weight_split_kernel(place, left, right, keep_ref, send_ref):
    split_rows(place, contract(left[...], right[0], 0, 0), keep_ref, send_ref, slice(None))


def heads_split_kernel(place, entry, qkv_grad, outer, mixed, keep_ref, send_ref):
    width = mixed.shape[-1]
    for kind in range(3):
        grad = contract(entry[...], qkv_grad[0, kind], 0, 0)
        split_rows(place, grad, keep_ref, send_ref, slice(kind * width, (kind + 1) * width))
    grad = contract(outer[...], mixed[0], 0, 0)
    split_rows(place, grad, keep_ref, send_ref, slice(3 * width, 4 * width))


def placed_call(kernel, place, steps, inputs, outputs, flops):
    shapes = [jax.ShapeDtypeStruct(shape, kind) for _, shape, kind in outputs]
    moved = sum(a.size * a.dtype.itemsize for _, a in inputs) + sum(
        s.size * s.dtype.itemsize for s in shapes
    )
    return pl.pallas_call(
        kernel,
        grid_spec=pltpu.PrefetchScalarGridSpec(
            num_scalar_prefetch=1,
            grid=(steps,),
            in_specs=[spec(array) for spec, array in inputs],
            out_specs=[spec(shape) for (spec, _, _), shape in zip(outputs, shapes)],
        ),
        out_shape=shapes,
        cost_estimate=pl.CostEstimate(flops=flops, transcendentals=0, bytes_accessed=moved),
        compiler_params=pltpu.CompilerParams(vmem_limit_bytes=56 << 20),
    )(place, *[array for _, array in inputs])


def resident(array):
    return pl.BlockSpec(
        array.shape, lambda step, place: (0,) * array.ndim, pipeline_mode=pl.Buffered(1)
    )


def by_first(array):
    rest = (0,) * (array.ndim - 1)
    return pl.BlockSpec((1,) + array.shape[1:], lambda step, place: (step,) + rest)


def to_first(array):
    rest = (0,) * (array.ndim - 1)
    return pl.BlockSpec(
        (1,) + array.shape[1:], lambda step, place: (jnp.bitwise_xor(step, place[1]),) + rest
    )


def by_second(array):
    shape = array.shape
    return pl.BlockSpec((shape[0], 1) + shape[2:], lambda step, place: (0, step, 0, 0))


def to_second(array):
    shape = array.shape
    return pl.BlockSpec(
        (shape[0], 1) + shape[2:], lambda step, place: (0, jnp.bitwise_xor(step, place[1]), 0, 0)
    )


def weight_grad(left, right, groups=1):
    batch, tokens, width = right.shape
    shape = (groups, batch, D // groups, width)
    return pl.pallas_call(
        weight_kernel,
        grid=(batch,),
        in_specs=[whole(left), pl.BlockSpec((1, tokens, width), lambda step: (step, 0, 0))],
        out_specs=pl.BlockSpec(
            (groups, 1, D // groups, width), lambda step: (0, step, 0, 0)
        ),
        out_shape=jax.ShapeDtypeStruct(shape, BF16),
        cost_estimate=pl.CostEstimate(
            flops=2 * D * batch * tokens * width, transcendentals=0, bytes_accessed=4 * D * batch * width
        ),
        compiler_params=pltpu.CompilerParams(vmem_limit_bytes=56 << 20),
    )(left, right)


def exchange(slots, axes):
    count, size = slots.shape
    rows = -(-size // 128)
    padded = jnp.pad(slots, ((0, 0), (0, rows * 128 - size))).reshape(count, rows, 128)
    return lax.all_to_all(padded, axes, 0, 0, tiled=True).reshape(count, -1)[:, :size]


def share(pieces, axes, count):
    row = jnp.concatenate([piece.astype(BF16).reshape(-1, 128) for piece in pieces])
    rows = row.shape[0]
    row = jnp.pad(row, ((0, -rows % 8), (0, 0)))
    return lax.all_to_all(
        jnp.broadcast_to(row[None], (count,) + row.shape), axes, 0, 0, tiled=True
    )[:, :rows]


def on_device(
    latents_in,
    condition,
    ada_weight,
    ada_bias,
    qkv_weight,
    qv_bias,
    proj_weight,
    proj_bias,
    hidden_weight,
    hidden_bias,
    down_weight,
    down_bias,
    upstream_grad,
    dp_size,
    tensor_size,
):
    axes = ("dp", "tensor")
    count = dp_size * tensor_size
    latents = condition.shape[0]
    tokens = latents_in.shape[0]
    ada_rows, ada_cols = ada_weight.shape[0], ada_bias.shape[0]
    here = lax.axis_index("dp") * tensor_size + lax.axis_index("tensor")
    place = lax.axis_index("tensor")
    slab = D // dp_size
    direct = dp_size == 8 and tensor_size == 4 and slab % 16 == 0
    head_width, hidden_width = qkv_weight.shape[2], hidden_weight.shape[1]

    silu_value, silu_pullback = jax.vjp(jax.nn.silu, condition.astype(F32))
    silu_cond = silu_value.astype(BF16)
    def packed_slots(weight, silu_rows):
        return jnp.concatenate(
            [
                weight.reshape(ada_rows, count, ada_cols).transpose(1, 0, 2).reshape(count, -1),
                silu_rows.reshape(latents, count, ada_rows).transpose(1, 0, 2).reshape(count, -1),
                jnp.broadcast_to(
                    jnp.concatenate([silu_rows.reshape(-1), qv_bias.reshape(-1), hidden_bias])[
                        None
                    ],
                    (count, latents * D + 2 * head_width + hidden_width),
                ),
            ],
            axis=1,
        )

    def swap(array, mask):
        return lax.ppermute(array, axes, [(device, device ^ mask) for device in range(count)])

    def slot(flows, inputs, run):
        moving = [[array for array, _ in flow.pending] for flow in flows]
        moving, inputs = lax.optimization_barrier((moving, inputs))
        results = [
            [swap(array, mask) for array, (_, mask) in zip(arrays, flow.pending)]
            for arrays, flow in zip(moving, flows)
        ]
        results, made = lax.optimization_barrier((results, run(*inputs)))
        for flow, arrived in zip(flows, results):
            flow.advance(arrived)
        return made

    across, along, upward = [tensor_size << bit for bit in range(3)]
    half = tensor_size // 2
    position = jnp.stack([lax.axis_index("dp"), place])

    def gather_stages(shard):
        line = yield [(shard, mask) for mask in range(1, tensor_size)]
        line = jnp.stack([shard] + line)
        side, above = yield [(line, along), (line, upward)]
        first, second = yield [(side[:half], upward), (above[half:], along)]
        own = jnp.stack([line, side, above, jnp.concatenate([first, second])])
        (other,) = yield [(own, across)]
        return own, other

    def reduce_stages(keep, send):
        (arrived,) = yield [(send, across)]
        summed = keep + arrived.astype(F32)
        line, side, above, far = [summed[number] for number in range(4)]
        moved = [
            jnp.concatenate(pair).astype(BF16)
            for pair in ((side[:half], far[:half]), (above[half:], far[half:]))
        ]
        arrived = yield list(zip(moved, (along, upward)))
        arrived = [block.astype(F32) for block in arrived]
        side_low, far_low = arrived[0][:half], arrived[0][half:]
        above_high, far_high = arrived[1][:half], arrived[1][half:]
        arrived = yield [
            ((above[:half] + far_low).astype(BF16), upward),
            ((side[half:] + far_high).astype(BF16), along),
        ]
        low = line[:half] + side_low + arrived[0].astype(F32)
        high = line[half:] + above_high + arrived[1].astype(F32)
        pieces = [low[number] for number in range(half)] + [high[number] for number in range(half)]
        arrived = yield [(pieces[mask].astype(BF16), mask) for mask in range(1, tensor_size)]
        return sum([block.astype(F32) for block in arrived], pieces[0])

    def gathered(shard):
        whole_set = lax.all_gather(shard, axes, axis=0)
        whole_set = whole_set.reshape((dp_size, tensor_size) + shard.shape)
        rows = whole_set.ndim - 2
        whole_set = jnp.moveaxis(whole_set, 0, rows - 1)
        return whole_set.reshape((1,) + whole_set.shape[: rows - 1] + (D, shard.shape[-1]))

    def scattered(blocks):
        blocks = blocks[0].reshape(-1, dp_size, slab, blocks.shape[-1]).swapaxes(0, 1)
        flat = blocks.reshape(-1, blocks.shape[-1])
        flat = lax.psum_scatter(flat, "dp", scatter_dimension=0, tiled=True)
        return lax.psum_scatter(flat, "tensor", scatter_dimension=0, tiled=True).astype(F32)

    def settled_heads(own, other):
        qkv_set, proj_set = placed_call(
            settle_heads_kernel,
            position,
            tensor_size,
            [(by_second, own), (by_second, other)],
            [
                (to_first, (tensor_size, 3, dp_size, slab, head_width), BF16),
                (to_first, (tensor_size, dp_size, slab, head_width), BF16),
            ],
            0,
        )
        return (
            qkv_set.reshape(1, tensor_size, 3, D, head_width),
            proj_set.reshape(1, tensor_size, D, head_width),
        )

    ends = [ada_rows * ada_cols]
    for size in (ada_rows * latents, latents * D, 2 * head_width):
        ends.append(ends[-1] + size)

    def opened(slots):
        got = exchange(slots, axes)
        columns = jnp.dot(
            got[:, ends[1] : ends[2]].reshape(count * latents, D),
            got[:, : ends[0]].reshape(D, ada_cols),
            preferred_element_type=F32,
        )
        columns = columns + ada_bias.astype(F32)
        return got, jnp.pad(
            columns.reshape(count, latents * ada_cols), ((0, 0), (0, -latents * ada_cols % 128))
        ).reshape(count, -1, 128)

    def modulate(columns):
        back = lax.all_to_all(columns, axes, 0, 0, tiled=True)
        back = back.reshape(count, -1)[:, : latents * ada_cols]
        return back.reshape(count, latents, ada_cols).transpose(1, 0, 2).reshape(latents, 6, D)

    heads_in = hidden_in = down_in = None
    if direct:
        heads_in, hidden_in, down_in = [
            Flow(gather_stages(shard))
            for shard in (
                jnp.concatenate(list(qkv_weight) + [proj_weight.T], axis=1),
                hidden_weight,
                down_weight.T,
            )
        ]
    sent = slot([heads_in] if direct else [], (ada_weight, silu_cond), packed_slots)
    got, columns = slot([heads_in, hidden_in] if direct else [], (sent,), opened)
    silu_columns = got[:, ends[0] : ends[1]].reshape(count * latents, ada_rows)
    qv_full = got[:tensor_size, ends[2] : ends[3]].reshape(tensor_size, 2, head_width)
    hidden_bias_full = got[:tensor_size, ends[3] :]
    modulation = slot(
        [heads_in, hidden_in, down_in] if direct else [], (columns,), modulate
    )
    if direct:
        slot([heads_in, hidden_in], (), lambda: ())
    else:
        qkv_full = gathered(qkv_weight)
        proj_full = gathered(proj_weight.T)
        hidden_full = gathered(hidden_weight)
        down_full = gathered(down_weight.T)

    def spread(*last):
        return (tensor_size,) + last

    unit = 2 * tokens * D * D

    def attend(first, steps):
        def run(rows, pieces, weight, bias, *kept_back):
            return over_latents(
                attend_kernel,
                steps,
                [(row_block, rows), (per_latent, pieces), (whole, weight), (whole, bias)],
                [
                    (row_block, (tokens, D), BF16),
                    (row_block, spread(3, tokens, head_width), BF16),
                    (row_block, spread(tokens, head_width), BF16),
                ],
                2 * unit * steps,
                first,
                kept_back,
            )

        return run

    def entered(rows, pieces, bias, *weights):
        weights = settled_heads(*weights)
        return attend(0, 1)(rows, pieces, weights[0], bias), weights

    if direct:
        carried, (qkv_full, proj_full) = slot(
            [down_in], (latents_in, modulation, qv_full) + heads_in.value, entered
        )
        for latent in range(1, latents):
            flows = [flow for flow in (hidden_in, down_in) if flow.value is None]
            carried = slot(
                flows,
                (latents_in, modulation, qkv_full, qv_full) + tuple(carried),
                attend(latent, 1),
            )
        while down_in.value is None:
            slot([down_in], (), lambda: ())
    else:
        carried = attend(0, latents)(latents_in, modulation, qkv_full, qv_full)
    input_one, qkv, mixed = carried
    (
        block_out,
        activated,
        preact_grad,
        mlp_grad,
        input_two,
        middle_grad,
        attended_grad,
        late_pieces,
        late_sums,
    ) = over_latents(
        block_settle_kernel if direct else block_kernel,
        latents,
        [
            (row_block, mixed),
            (row_block, latents_in),
            (row_block, upstream_grad),
            (per_latent, modulation),
            (whole, proj_full),
            (whole, proj_bias[None]),
        ]
        + [(whole, array) for array in (hidden_in.value if direct else (hidden_full,))]
        + [(whole, hidden_bias_full)]
        + [(whole, array) for array in (down_in.value if direct else (down_full,))]
        + [(whole, down_bias[None])]
        + ([(scalars, position)] if direct else []),
        [
            (row_block, (tokens, D), F32),
            (row_block, spread(tokens, hidden_width), BF16),
            (row_block, spread(tokens, hidden_width), BF16),
            (row_block, (tokens, D), BF16),
            (row_block, (tokens, D), BF16),
            (row_block, (tokens, D), F32),
            (row_block, (tokens, D), BF16),
            (per_latent, (latents, 4, D), F32),
            (kept, (tensor_size + 2, D), F32),
        ],
        18 * unit,
        scratch=[pltpu.VMEM((dp_size, tensor_size, slab, D), BF16)] * 2 if direct else (),
    )

    split_shape = (dp_size // 2, tensor_size, slab, D)
    split_out = [(to_second, split_shape, F32), (to_second, split_shape, BF16)]

    def square_grad(left, right):
        return placed_call(
            weight_split_kernel,
            position,
            tensor_size,
            [(resident, left), (by_first, right)],
            split_out,
            4 * unit,
        )

    def heads_grad(entry, heads, outer, inner):
        return placed_call(
            heads_split_kernel,
            position,
            tensor_size,
            [(resident, entry), (by_first, heads), (resident, outer), (by_first, inner)],
            split_out,
            4 * unit,
        )

    def latent_back(first, steps, carried):
        def run(outer, heads, proj, weight, rows, pieces, middle, *kept_back):
            return over_latents(
                latent_back_kernel,
                steps,
                [
                    (row_block, outer),
                    (row_block, heads),
                    (whole, proj),
                    (whole, weight),
                    (row_block, rows),
                    (per_latent, pieces),
                    (row_block, middle),
                ],
                [
                    (row_block, spread(3, tokens, head_width), BF16),
                    (row_block, (tokens, D), F32),
                    (per_latent, (latents, 2, D), F32),
                    (kept, spread(3, head_width), F32),
                ],
                6 * unit * steps,
                first,
                kept_back,
            )

        inputs = (attended_grad, qkv, proj_full, qkv_full, latents_in, modulation, middle_grad)
        return inputs + carried, run

    vector_rows = latents * 6 * D // 128

    def vectors(early, late, sums, head_sums):
        row = jnp.concatenate(
            [
                piece.astype(BF16).reshape(-1, 128)
                for piece in (jnp.concatenate([early, late], axis=1), sums, head_sums[:, ::2])
            ]
        )
        return jnp.pad(row, ((0, -row.shape[0] % 16), (0, 0)))

    def modulation_of(shared):
        return shared[:, :vector_rows].reshape(count * latents, 6 * D)

    def ada_back(shared, silu_columns, to_owner):
        modulation_all = modulation_of(shared)
        slots = contract(modulation_all, ada_weight, 1, 1).reshape(count, latents * ada_rows)
        slots = jnp.dot(to_owner, slots, precision=lax.Precision.HIGHEST)
        return exchange(slots, axes), contract(silu_columns, modulation_all, 0, 0)

    def condition_back(slots):
        grad = slots.reshape(count, latents, ada_rows).transpose(1, 0, 2).reshape(latents, D)
        return silu_pullback(grad)[0]

    numbers = lax.broadcasted_iota(jnp.int32, (count, count), 0)
    order = lax.broadcasted_iota(jnp.int32, (count, count), 1)
    if direct:
        plane, cell = order // (count // 2), order % (count // 2)
        pair, line = cell // tensor_size, cell % tensor_size
        order = jnp.bitwise_xor(2 * pair + plane, position[0]) * tensor_size + jnp.bitwise_xor(
            line, position[1]
        )
    to_owner = (numbers == order).astype(F32)
    silu_columns = contract(
        to_owner.astype(BF16), silu_columns.reshape(count, latents * ada_rows), 0, 0
    )
    silu_columns = silu_columns.astype(BF16).reshape(count * latents, ada_rows)

    if direct:
        down_out = Flow(reduce_stages(*square_grad(mlp_grad, activated)))
        hidden_out = Flow(
            reduce_stages(*slot([down_out], (input_two, preact_grad), square_grad))
        )
        qkv_sums, carried = 0.0, ()
        for latent in range(latents):
            flows = [flow for flow in (down_out, hidden_out) if flow.value is None]
            *carried, own_sums = slot(flows, *latent_back(latent, 1, tuple(carried)))
            qkv_sums = qkv_sums + own_sums
        qkv_grad, input_grad, early_pieces = carried
        shared_in = Flow(
            gather_stages(vectors(early_pieces, late_pieces, late_sums, qkv_sums))
        )
        flows = [flow for flow in (down_out, hidden_out) if flow.value is None]
        heads_out = Flow(
            reduce_stages(
                *slot(
                    flows + [shared_in], (input_one, qkv_grad, attended_grad, mixed), heads_grad
                )
            )
        )
        for _ in range(3):
            slot([heads_out, shared_in], (), lambda: ())
        shared = jnp.stack(shared_in.value).reshape(count, -1, 128)
        silu_grad, ada_weight_grad = slot(
            [heads_out], (shared, silu_columns, to_owner), ada_back
        )
        condition_grad = condition_back(silu_grad)
        down_weight_grad, hidden_weight_grad = down_out.value.T, hidden_out.value
        packed_grad = heads_out.value.reshape(slab, 4, head_width)
        qkv_weight_grad = packed_grad[:, :3].swapaxes(0, 1)
        proj_weight_grad = packed_grad[:, 3].T
    else:
        inputs, run = latent_back(0, latents, ())
        qkv_grad, input_grad, early_pieces, qkv_sums = run(*inputs)
        down_weight_grad = scattered(weight_grad(mlp_grad, activated)).T
        hidden_weight_grad = scattered(weight_grad(input_two, preact_grad))
        proj_weight_grad = scattered(weight_grad(attended_grad, mixed)).T
        qkv_weight_grad = scattered(
            weight_grad(input_one, qkv_grad.reshape(-1, tokens, head_width))
        ).reshape(qkv_weight.shape)
        shared = share([vectors(early_pieces, late_pieces, late_sums, qkv_sums)], axes, count)
        silu_grad, ada_weight_grad = ada_back(shared, silu_columns, to_owner)
        condition_grad = condition_back(silu_grad)
    totals = jnp.sum(shared[:, vector_rows:].astype(F32), axis=0).reshape(-1)
    sums_end = (tensor_size + 2) * D
    rest = totals[:sums_end].reshape(tensor_size + 2, D)
    qv_bias_grad = lax.dynamic_index_in_dim(
        totals[sums_end : sums_end + 2 * D].reshape(tensor_size, 2, head_width),
        place,
        0,
        keepdims=False,
    )
    hidden_bias_grad = lax.dynamic_index_in_dim(rest, place, 0, keepdims=False)
    proj_bias_grad, down_bias_grad = rest[tensor_size], rest[tensor_size + 1]
    ada_bias_grad = lax.dynamic_index_in_dim(
        jnp.sum(modulation_of(shared).astype(F32), axis=0).reshape(count, ada_cols),
        here,
        0,
        keepdims=False,
    )
    return (
        block_out,
        input_grad,
        condition_grad,
        ada_weight_grad,
        ada_bias_grad,
        qkv_weight_grad,
        qv_bias_grad,
        proj_weight_grad,
        proj_bias_grad,
        hidden_weight_grad,
        hidden_bias_grad,
        down_weight_grad,
        down_bias_grad,
    )


def solution(mesh):
    both = ("dp", "tensor")
    placed = (
        P(both, None),
        P(both, None),
        P(both, None),
        P(both),
        P(None, "dp", "tensor"),
        P(None, "tensor"),
        P("tensor", "dp"),
        P(),
        P("dp", "tensor"),
        P("tensor"),
        P("tensor", "dp"),
        P(),
        P(both, None),
    )
    return jax.shard_map(
        functools.partial(
            on_device, dp_size=mesh.shape["dp"], tensor_size=mesh.shape["tensor"]
        ),
        mesh=mesh,
        in_specs=placed,
        out_specs=(P(both, None), P(both, None)) + placed[1:-1],
        check_vma=False,
    )
```

```python
import functools

import jax
import jax.numpy as jnp
from jax import lax
from jax.experimental import pallas as pl
from jax.experimental.pallas import tpu as pltpu
from jax.sharding import PartitionSpec as P

D = 768
HD = 64
SEQ = 256
BF16 = jnp.bfloat16
F32 = jnp.float32


def normalize_rows(values):
    centre = values - jnp.mean(values, axis=-1, keepdims=True)
    inverse = lax.rsqrt(jnp.mean(centre * centre, axis=-1, keepdims=True) + 1e-06)
    return (centre * inverse, inverse)


def norm_backward(grad_normed, normed, inverse):
    return inverse * (
        grad_normed
        - jnp.mean(grad_normed, axis=-1, keepdims=True)
        - normed * jnp.mean(grad_normed * normed, axis=-1, keepdims=True)
    )


def contract(left, right, left_axis, right_axis):
    return lax.dot_general(
        left, right, (((left_axis,), (right_axis,)), ((), ())), preferred_element_type=F32
    )


def matrix(ref, *place):
    block = ref[(slice(None),) + place]
    return block.reshape(-1, block.shape[-1])


def column_sum(values):
    return jnp.sum(values, axis=0, keepdims=True)


def head_masks(width):
    lanes = lax.broadcasted_iota(jnp.int32, (1, width), 1)
    return [
        ((lanes >= start) & (lanes < start + HD)).astype(F32).astype(BF16)
        for start in range(0, width, HD)
    ]


def head_probs(query, key):
    scores = contract(query, key, 1, 1) * HD ** (-0.5)
    raised = jnp.exp(scores - jnp.max(scores, axis=-1, keepdims=True))
    return raised * (1.0 / jnp.sum(raised, axis=-1, keepdims=True))


def attend_kernel(rows, modulation, weight, bias, input_ref, qkv_ref, mixed_ref):
    normed, _ = normalize_rows(rows[...].astype(F32))
    pieces = modulation[0]
    inputs = (normed * (1.0 + pieces[1:2]) + pieces[0:1]).astype(BF16)
    input_ref[...] = inputs
    masks = head_masks(qkv_ref.shape[-1])
    for part in range(qkv_ref.shape[0]):
        query = (contract(inputs, matrix(weight, part, 0), 1, 0) + bias[part, 0:1].astype(F32)).astype(BF16)
        key = contract(inputs, matrix(weight, part, 1), 1, 0).astype(BF16)
        value = (contract(inputs, matrix(weight, part, 2), 1, 0) + bias[part, 1:2].astype(F32)).astype(BF16)
        qkv_ref[part, 0] = query
        qkv_ref[part, 1] = key
        qkv_ref[part, 2] = value
        mixed = None
        for mask in masks:
            probs = head_probs(query * mask, key).astype(BF16)
            own = contract(probs, value * mask, 1, 0)
            mixed = own if mixed is None else mixed + own
        mixed_ref[part] = mixed.astype(BF16)


def block_kernel(
    mixed,
    rows,
    upstream_rows,
    modulation,
    proj,
    proj_bias,
    hidden,
    hidden_bias,
    down,
    down_bias,
    out_ref,
    act_ref,
    preact_grad_ref,
    mlp_grad_ref,
    input_ref,
    middle_grad_ref,
    attended_grad_ref,
    pieces_ref,
    sums_ref,
):
    parts = act_ref.shape[0]
    pieces = modulation[0]
    gate_one, shift_two, scale_two, gate_two = [pieces[k : k + 1] for k in (2, 3, 4, 5)]
    attended = proj_bias[...].astype(F32)
    for part in range(parts):
        attended = attended + contract(mixed[part], matrix(proj, part), 1, 1)
    middle = rows[...].astype(F32) + gate_one * attended
    normed, inverse = normalize_rows(middle)
    inputs = (normed * (1.0 + scale_two) + shift_two).astype(BF16)
    input_ref[...] = inputs
    upstream = upstream_rows[...].astype(F32)
    mlp_grad = (gate_two * upstream).astype(BF16)
    mlp_grad_ref[...] = mlp_grad

    @pl.when(pl.program_id(0) == 0)
    def _():
        sums_ref[...] = jnp.zeros_like(sums_ref)

    mlp = down_bias[...].astype(F32)
    input_grad = None
    root = 0.7978845608028654
    for part in range(parts):
        hidden_part = matrix(hidden, part)
        down_part = matrix(down, part)
        preact = contract(inputs, hidden_part, 1, 0) + hidden_bias[part : part + 1].astype(F32)
        square = preact * preact
        bent = jnp.tanh(root * preact * (1.0 + 0.044715 * square))
        half = 0.5 + 0.5 * bent
        activated = (preact * half).astype(BF16)
        slope = half + (0.5 * root) * preact * (1.0 - bent * bent) * (1.0 + (3 * 0.044715) * square)
        act_ref[part] = activated
        mlp = mlp + contract(activated, down_part, 1, 1)
        preact_grad = (contract(mlp_grad, down_part, 1, 0) * slope).astype(BF16)
        preact_grad_ref[part] = preact_grad
        sums_ref[part : part + 1] += column_sum(preact_grad.astype(F32))
        own = contract(preact_grad, hidden_part, 1, 1)
        input_grad = own if input_grad is None else input_grad + own
    out_ref[...] = middle + gate_two * mlp
    middle_grad = upstream + norm_backward(input_grad * (1.0 + scale_two), normed, inverse)
    middle_grad_ref[...] = middle_grad
    attended_grad = (gate_one * middle_grad).astype(BF16)
    attended_grad_ref[...] = attended_grad
    pieces_ref[0, 0:1] = column_sum(middle_grad * attended)
    pieces_ref[0, 1:2] = column_sum(input_grad)
    pieces_ref[0, 2:3] = column_sum(input_grad * normed)
    pieces_ref[0, 3:4] = column_sum(upstream * mlp)
    sums_ref[parts : parts + 1] += column_sum(attended_grad.astype(F32))
    sums_ref[parts + 1 : parts + 2] += column_sum(mlp_grad.astype(F32))


def block_settle_kernel(
    mixed,
    rows,
    upstream_rows,
    modulation,
    proj,
    proj_bias,
    hidden_own,
    hidden_other,
    hidden_bias,
    down_own,
    down_other,
    down_bias,
    place,
    *refs,
):
    made, (hidden, down) = refs[:-2], refs[-2:]

    @pl.when(pl.program_id(0) == 0)
    def _():
        for number in range(hidden.shape[1]):
            line = jnp.bitwise_xor(number, place[1])
            for pair in range(hidden_own.shape[0]):
                for core, sources in enumerate(
                    ((hidden_own, down_own), (hidden_other, down_other))
                ):
                    spot = jnp.bitwise_xor(2 * pair + core, place[0])
                    hidden[spot, line] = sources[0][pair, number]
                    down[spot, line] = sources[1][pair, number]

    block_kernel(
        mixed,
        rows,
        upstream_rows,
        modulation,
        proj,
        proj_bias,
        hidden,
        hidden_bias,
        down,
        down_bias,
        *made,
    )


def attend_back_kernel(attended_grad, qkv, proj, grad_ref, sums_ref):
    width = qkv.shape[-1]
    masks = head_masks(width)

    @pl.when(pl.program_id(0) == 0)
    def _():
        sums_ref[...] = jnp.zeros_like(sums_ref)

    for part in range(qkv.shape[0]):
        query, key, value = qkv[part, 0], qkv[part, 1], qkv[part, 2]
        mixed_grad = contract(attended_grad[...], matrix(proj, part), 1, 0).astype(BF16)
        totals = [None, None, None]
        for mask in masks:
            own_query, own_grad = query * mask, mixed_grad * mask
            probs = head_probs(own_query, key)
            probs_grad = contract(own_grad, value, 1, 1)
            scores_grad = (
                probs * (probs_grad - jnp.sum(probs * probs_grad, axis=-1, keepdims=True))
            ).astype(BF16)
            own = (
                contract(scores_grad, key * mask, 1, 0),
                contract(scores_grad, own_query, 0, 0),
                contract(probs.astype(BF16), own_grad, 0, 0),
            )
            totals = [new if old is None else old + new for old, new in zip(totals, own)]
        for kind, factor in enumerate((HD ** (-0.5), HD ** (-0.5), 1.0)):
            low = (totals[kind] * factor).astype(BF16)
            grad_ref[part, kind] = low
            sums_ref[part, kind : kind + 1] += column_sum(low.astype(F32))


def entry_back_kernel(qkv_grad, weight, rows, modulation, middle_grad, grad_ref, pieces_ref):
    input_grad = None
    for part in range(qkv_grad.shape[0]):
        for kind in range(3):
            own = contract(qkv_grad[part, kind], matrix(weight, part, kind), 1, 1)
            input_grad = own if input_grad is None else input_grad + own
    normed, inverse = normalize_rows(rows[...].astype(F32))
    pieces = modulation[0]
    grad_ref[...] = middle_grad[...] + norm_backward(
        input_grad * (1.0 + pieces[1:2]), normed, inverse
    )
    pieces_ref[0, 0:1] = column_sum(input_grad)
    pieces_ref[0, 1:2] = column_sum(input_grad * normed)


def weight_kernel(left, right, grad_ref):
    grad = contract(left[...], right[0], 0, 0)
    grad_ref[:, 0] = grad.reshape(grad_ref.shape[0], grad_ref.shape[2], -1).astype(BF16)


def whole(array, first=0):
    return pl.BlockSpec(
        array.shape, lambda step: (0,) * array.ndim, pipeline_mode=pl.Buffered(1)
    )


def row_block(array, first=0):
    lead = array.shape[:-2]
    return pl.BlockSpec(
        lead + (SEQ, array.shape[-1]), lambda step: (0,) * len(lead) + (step + first, 0)
    )


def per_latent(array, first=0):
    return pl.BlockSpec((1,) + array.shape[1:], lambda step: (step + first, 0, 0))


def scalars(array, first=0):
    return pl.BlockSpec(memory_space=pltpu.SMEM)


def kept(array, first=0):
    return pl.BlockSpec(array.shape, lambda step: (0,) * array.ndim)


def over_latents(kernel, steps, inputs, outputs, flops, first=0, carried=(), scratch=()):
    shapes = [jax.ShapeDtypeStruct(shape, kind) for _, shape, kind in outputs]
    moved = sum(a.size * a.dtype.itemsize for _, a in inputs) + sum(
        s.size * s.dtype.itemsize for s in shapes
    )
    taken = len(inputs)

    def body(*refs):
        kernel(*refs[:taken], *refs[taken + len(carried) :])

    return pl.pallas_call(
        body,
        grid=(steps,),
        in_specs=[spec(array, first) for spec, array in inputs]
        + [pl.BlockSpec(memory_space=pl.ANY) for _ in carried],
        out_specs=[spec(shape, first) for (spec, _, _), shape in zip(outputs, shapes)],
        out_shape=shapes,
        scratch_shapes=list(scratch),
        input_output_aliases={taken + number: number for number in range(len(carried))},
        cost_estimate=pl.CostEstimate(flops=flops, transcendentals=0, bytes_accessed=moved),
        compiler_params=pltpu.CompilerParams(vmem_limit_bytes=56 << 20),
    )(*[array for _, array in inputs], *carried)


class Flow:
    def __init__(self, stages):
        self.stages = stages
        self.pending = next(stages)
        self.value = None

    def advance(self, results):
        try:
            self.pending = self.stages.send(results)
        except StopIteration as end:
            self.value = end.value


def settle_heads_kernel(place, own, other, qkv_ref, proj_ref):
    flip = place[0]
    width = proj_ref.shape[-1]
    for pair in range(own.shape[0]):
        for core, source in enumerate((own, other)):
            slot = jnp.bitwise_xor(2 * pair + core, flip)
            block = source[pair, 0]
            for kind in range(3):
                qkv_ref[0, kind, slot] = block[:, kind * width : (kind + 1) * width]
            proj_ref[0, slot] = block[:, 3 * width :]


def latent_back_kernel(
    attended_grad,
    qkv,
    proj,
    weight,
    rows,
    modulation,
    middle_grad,
    heads_ref,
    grad_ref,
    pieces_ref,
    sums_ref,
):
    attend_back_kernel(attended_grad, qkv, proj, heads_ref, sums_ref)
    entry_back_kernel(heads_ref, weight, rows, modulation, middle_grad, grad_ref, pieces_ref)


def split_rows(place, grad, keep_ref, send_ref, lanes):
    slab = keep_ref.shape[2]
    core = jnp.bitwise_and(place[0], 1)
    flip = place[0] // 2
    for pair in range(keep_ref.shape[0]):
        low = grad[2 * pair * slab : (2 * pair + 1) * slab]
        high = grad[(2 * pair + 1) * slab : (2 * pair + 2) * slab]
        slot = jnp.bitwise_xor(pair, flip)
        keep_ref[slot, 0, :, lanes] = jnp.where(core == 0, low, high).astype(BF16)
        send_ref[slot, 0, :, lanes] = jnp.where(core == 0, high, low).astype(BF16)


def weight_split_kernel(place, left, right, keep_ref, send_ref):
    split_rows(place, contract(left[...], right[0], 0, 0), keep_ref, send_ref, slice(None))


def heads_split_kernel(place, entry, qkv_grad, outer, mixed, keep_ref, send_ref):
    width = mixed.shape[-1]
    for kind in range(3):
        grad = contract(entry[...], qkv_grad[0, kind], 0, 0)
        split_rows(place, grad, keep_ref, send_ref, slice(kind * width, (kind + 1) * width))
    grad = contract(outer[...], mixed[0], 0, 0)
    split_rows(place, grad, keep_ref, send_ref, slice(3 * width, 4 * width))


def placed_call(kernel, place, steps, inputs, outputs, flops):
    shapes = [jax.ShapeDtypeStruct(shape, kind) for _, shape, kind in outputs]
    moved = sum(a.size * a.dtype.itemsize for _, a in inputs) + sum(
        s.size * s.dtype.itemsize for s in shapes
    )
    return pl.pallas_call(
        kernel,
        grid_spec=pltpu.PrefetchScalarGridSpec(
            num_scalar_prefetch=1,
            grid=(steps,),
            in_specs=[spec(array) for spec, array in inputs],
            out_specs=[spec(shape) for (spec, _, _), shape in zip(outputs, shapes)],
        ),
        out_shape=shapes,
        cost_estimate=pl.CostEstimate(flops=flops, transcendentals=0, bytes_accessed=moved),
        compiler_params=pltpu.CompilerParams(vmem_limit_bytes=56 << 20),
    )(place, *[array for _, array in inputs])


def resident(array):
    return pl.BlockSpec(
        array.shape, lambda step, place: (0,) * array.ndim, pipeline_mode=pl.Buffered(1)
    )


def by_first(array):
    rest = (0,) * (array.ndim - 1)
    return pl.BlockSpec((1,) + array.shape[1:], lambda step, place: (step,) + rest)


def to_first(array):
    rest = (0,) * (array.ndim - 1)
    return pl.BlockSpec(
        (1,) + array.shape[1:], lambda step, place: (jnp.bitwise_xor(step, place[1]),) + rest
    )


def by_second(array):
    shape = array.shape
    return pl.BlockSpec((shape[0], 1) + shape[2:], lambda step, place: (0, step, 0, 0))


def to_second(array):
    shape = array.shape
    return pl.BlockSpec(
        (shape[0], 1) + shape[2:], lambda step, place: (0, jnp.bitwise_xor(step, place[1]), 0, 0)
    )


def weight_grad(left, right, groups=1):
    batch, tokens, width = right.shape
    shape = (groups, batch, D // groups, width)
    return pl.pallas_call(
        weight_kernel,
        grid=(batch,),
        in_specs=[whole(left), pl.BlockSpec((1, tokens, width), lambda step: (step, 0, 0))],
        out_specs=pl.BlockSpec(
            (groups, 1, D // groups, width), lambda step: (0, step, 0, 0)
        ),
        out_shape=jax.ShapeDtypeStruct(shape, BF16),
        cost_estimate=pl.CostEstimate(
            flops=2 * D * batch * tokens * width, transcendentals=0, bytes_accessed=4 * D * batch * width
        ),
        compiler_params=pltpu.CompilerParams(vmem_limit_bytes=56 << 20),
    )(left, right)


def exchange(slots, axes):
    count, size = slots.shape
    rows = -(-size // 128)
    padded = jnp.pad(slots, ((0, 0), (0, rows * 128 - size))).reshape(count, rows, 128)
    return lax.all_to_all(padded, axes, 0, 0, tiled=True).reshape(count, -1)[:, :size]


def share(pieces, axes, count):
    row = jnp.concatenate([piece.astype(BF16).reshape(-1, 128) for piece in pieces])
    rows = row.shape[0]
    row = jnp.pad(row, ((0, -rows % 8), (0, 0)))
    return lax.all_to_all(
        jnp.broadcast_to(row[None], (count,) + row.shape), axes, 0, 0, tiled=True
    )[:, :rows]


def on_device(
    latents_in,
    condition,
    ada_weight,
    ada_bias,
    qkv_weight,
    qv_bias,
    proj_weight,
    proj_bias,
    hidden_weight,
    hidden_bias,
    down_weight,
    down_bias,
    upstream_grad,
    dp_size,
    tensor_size,
):
    axes = ("dp", "tensor")
    count = dp_size * tensor_size
    latents = condition.shape[0]
    tokens = latents_in.shape[0]
    ada_rows, ada_cols = ada_weight.shape[0], ada_bias.shape[0]
    here = lax.axis_index("dp") * tensor_size + lax.axis_index("tensor")
    place = lax.axis_index("tensor")
    slab = D // dp_size
    direct = dp_size == 8 and tensor_size == 4 and slab % 16 == 0
    head_width, hidden_width = qkv_weight.shape[2], hidden_weight.shape[1]

    silu_value, silu_pullback = jax.vjp(jax.nn.silu, condition.astype(F32))
    silu_cond = silu_value.astype(BF16)
    def packed_slots(weight, silu_rows):
        return jnp.concatenate(
            [
                weight.reshape(ada_rows, count, ada_cols).transpose(1, 0, 2).reshape(count, -1),
                silu_rows.reshape(latents, count, ada_rows).transpose(1, 0, 2).reshape(count, -1),
                jnp.broadcast_to(
                    jnp.concatenate([silu_rows.reshape(-1), qv_bias.reshape(-1), hidden_bias])[
                        None
                    ],
                    (count, latents * D + 2 * head_width + hidden_width),
                ),
            ],
            axis=1,
        )

    def swap(array, mask):
        return lax.ppermute(array, axes, [(device, device ^ mask) for device in range(count)])

    def slot(flows, inputs, run):
        moving = [[array for array, _ in flow.pending] for flow in flows]
        moving, inputs = lax.optimization_barrier((moving, inputs))
        results = [
            [swap(array, mask) for array, (_, mask) in zip(arrays, flow.pending)]
            for arrays, flow in zip(moving, flows)
        ]
        results, made = lax.optimization_barrier((results, run(*inputs)))
        for flow, arrived in zip(flows, results):
            flow.advance(arrived)
        return made

    across, along, upward = [tensor_size << bit for bit in range(3)]
    half = tensor_size // 2
    position = jnp.stack([lax.axis_index("dp"), place])

    def gather_stages(shard):
        line = yield [(shard, mask) for mask in range(1, tensor_size)]
        line = jnp.stack([shard] + line)
        side, above = yield [(line, along), (line, upward)]
        first, second = yield [(side[:half], upward), (above[half:], along)]
        own = jnp.stack([line, side, above, jnp.concatenate([first, second])])
        (other,) = yield [(own, across)]
        return own, other

    def vector_stages(row):
        line = yield [(row, mask) for mask in range(1, tensor_size)]
        line = jnp.stack([row] + line)
        near = yield [(line, along), (line, upward), (line, along + upward)]
        return jnp.stack([line] + near)

    def reduce_stages(keep, send):
        (arrived,) = yield [(send, across)]
        summed = keep.astype(F32) + arrived.astype(F32)
        line, side, above, far = [summed[number] for number in range(4)]
        moved = [
            jnp.concatenate(pair).astype(BF16)
            for pair in ((side[:half], far[:half]), (above[half:], far[half:]))
        ]
        arrived = yield list(zip(moved, (along, upward)))
        arrived = [block.astype(F32) for block in arrived]
        side_low, far_low = arrived[0][:half], arrived[0][half:]
        above_high, far_high = arrived[1][:half], arrived[1][half:]
        arrived = yield [
            ((above[:half] + far_low).astype(BF16), upward),
            ((side[half:] + far_high).astype(BF16), along),
        ]
        low = line[:half] + side_low + arrived[0].astype(F32)
        high = line[half:] + above_high + arrived[1].astype(F32)
        pieces = [low[number] for number in range(half)] + [high[number] for number in range(half)]
        arrived = yield [(pieces[mask].astype(BF16), mask) for mask in range(1, tensor_size)]
        return sum([block.astype(F32) for block in arrived], pieces[0])

    def gathered(shard):
        whole_set = lax.all_gather(shard, axes, axis=0)
        whole_set = whole_set.reshape((dp_size, tensor_size) + shard.shape)
        rows = whole_set.ndim - 2
        whole_set = jnp.moveaxis(whole_set, 0, rows - 1)
        return whole_set.reshape((1,) + whole_set.shape[: rows - 1] + (D, shard.shape[-1]))

    def scattered(blocks):
        blocks = blocks[0].reshape(-1, dp_size, slab, blocks.shape[-1]).swapaxes(0, 1)
        flat = blocks.reshape(-1, blocks.shape[-1])
        flat = lax.psum_scatter(flat, "dp", scatter_dimension=0, tiled=True)
        return lax.psum_scatter(flat, "tensor", scatter_dimension=0, tiled=True).astype(F32)

    def settled_heads(own, other):
        qkv_set, proj_set = placed_call(
            settle_heads_kernel,
            position,
            tensor_size,
            [(by_second, own), (by_second, other)],
            [
                (to_first, (tensor_size, 3, dp_size, slab, head_width), BF16),
                (to_first, (tensor_size, dp_size, slab, head_width), BF16),
            ],
            0,
        )
        return (
            qkv_set.reshape(1, tensor_size, 3, D, head_width),
            proj_set.reshape(1, tensor_size, D, head_width),
        )

    ends = [ada_rows * ada_cols]
    for size in (ada_rows * latents, latents * D, 2 * head_width):
        ends.append(ends[-1] + size)

    def modulate(columns):
        back = lax.all_to_all(columns, axes, 0, 0, tiled=True)
        back = back.reshape(count, -1)[:, : latents * ada_cols]
        return back.reshape(count, latents, ada_cols).transpose(1, 0, 2).reshape(latents, 6, D)

    def opened(slots):
        got = exchange(slots, axes)
        columns = jnp.dot(
            got[:, ends[1] : ends[2]].reshape(count * latents, D),
            got[:, : ends[0]].reshape(D, ada_cols),
            preferred_element_type=F32,
        )
        columns = columns + ada_bias.astype(F32)
        columns = jnp.pad(
            columns.reshape(count, latents * ada_cols), ((0, 0), (0, -latents * ada_cols % 128))
        ).reshape(count, -1, 128)
        return got, modulate(columns)

    heads_in = hidden_in = down_in = None
    if direct:
        heads_in, hidden_in, down_in = [
            Flow(gather_stages(shard))
            for shard in (
                jnp.concatenate(list(qkv_weight) + [proj_weight.T], axis=1),
                hidden_weight,
                down_weight.T,
            )
        ]
    sent = slot([heads_in] if direct else [], (ada_weight, silu_cond), packed_slots)
    got, modulation = slot([heads_in, hidden_in] if direct else [], (sent,), opened)
    silu_columns = got[:, ends[0] : ends[1]].reshape(count * latents, ada_rows)
    qv_full = got[:tensor_size, ends[2] : ends[3]].reshape(tensor_size, 2, head_width)
    hidden_bias_full = got[:tensor_size, ends[3] :]
    if direct:
        slot([heads_in, hidden_in, down_in], (), lambda: ())
        slot([heads_in, hidden_in], (), lambda: ())
    else:
        qkv_full = gathered(qkv_weight)
        proj_full = gathered(proj_weight.T)
        hidden_full = gathered(hidden_weight)
        down_full = gathered(down_weight.T)

    def spread(*last):
        return (tensor_size,) + last

    unit = 2 * tokens * D * D

    def attend(first, steps):
        def run(rows, pieces, weight, bias, *kept_back):
            return over_latents(
                attend_kernel,
                steps,
                [(row_block, rows), (per_latent, pieces), (whole, weight), (whole, bias)],
                [
                    (row_block, (tokens, D), BF16),
                    (row_block, spread(3, tokens, head_width), BF16),
                    (row_block, spread(tokens, head_width), BF16),
                ],
                2 * unit * steps,
                first,
                kept_back,
            )

        return run

    def entered(rows, pieces, bias, *weights):
        weights = settled_heads(*weights)
        return attend(0, 1)(rows, pieces, weights[0], bias), weights

    if direct:
        carried, (qkv_full, proj_full) = slot(
            [down_in], (latents_in, modulation, qv_full) + heads_in.value, entered
        )
        for latent in range(1, latents):
            flows = [flow for flow in (hidden_in, down_in) if flow.value is None]
            carried = slot(
                flows,
                (latents_in, modulation, qkv_full, qv_full) + tuple(carried),
                attend(latent, 1),
            )
        while down_in.value is None:
            slot([down_in], (), lambda: ())
    else:
        carried = attend(0, latents)(latents_in, modulation, qkv_full, qv_full)
    input_one, qkv, mixed = carried
    (
        block_out,
        activated,
        preact_grad,
        mlp_grad,
        input_two,
        middle_grad,
        attended_grad,
        late_pieces,
        late_sums,
    ) = over_latents(
        block_settle_kernel if direct else block_kernel,
        latents,
        [
            (row_block, mixed),
            (row_block, latents_in),
            (row_block, upstream_grad),
            (per_latent, modulation),
            (whole, proj_full),
            (whole, proj_bias[None]),
        ]
        + [(whole, array) for array in (hidden_in.value if direct else (hidden_full,))]
        + [(whole, hidden_bias_full)]
        + [(whole, array) for array in (down_in.value if direct else (down_full,))]
        + [(whole, down_bias[None])]
        + ([(scalars, position)] if direct else []),
        [
            (row_block, (tokens, D), F32),
            (row_block, spread(tokens, hidden_width), BF16),
            (row_block, spread(tokens, hidden_width), BF16),
            (row_block, (tokens, D), BF16),
            (row_block, (tokens, D), BF16),
            (row_block, (tokens, D), F32),
            (row_block, (tokens, D), BF16),
            (per_latent, (latents, 4, D), F32),
            (kept, (tensor_size + 2, D), F32),
        ],
        18 * unit,
        scratch=[pltpu.VMEM((dp_size, tensor_size, slab, D), BF16)] * 2 if direct else (),
    )

    split_shape = (dp_size // 2, tensor_size, slab, D)
    split_out = [(to_second, split_shape, BF16), (to_second, split_shape, BF16)]

    def square_grad(left, right):
        return placed_call(
            weight_split_kernel,
            position,
            tensor_size,
            [(resident, left), (by_first, right)],
            split_out,
            4 * unit,
        )

    def heads_grad(entry, heads, outer, inner):
        return placed_call(
            heads_split_kernel,
            position,
            tensor_size,
            [(resident, entry), (by_first, heads), (resident, outer), (by_first, inner)],
            split_out,
            4 * unit,
        )

    def latent_back(first, steps, carried):
        def run(outer, heads, proj, weight, rows, pieces, middle, *kept_back):
            return over_latents(
                latent_back_kernel,
                steps,
                [
                    (row_block, outer),
                    (row_block, heads),
                    (whole, proj),
                    (whole, weight),
                    (row_block, rows),
                    (per_latent, pieces),
                    (row_block, middle),
                ],
                [
                    (row_block, spread(3, tokens, head_width), BF16),
                    (row_block, (tokens, D), F32),
                    (per_latent, (latents, 2, D), F32),
                    (kept, spread(3, head_width), F32),
                ],
                6 * unit * steps,
                first,
                kept_back,
            )

        inputs = (attended_grad, qkv, proj_full, qkv_full, latents_in, modulation, middle_grad)
        return inputs + carried, run

    vector_rows = latents * 6 * D // 128

    def vectors(early, late, sums, head_sums):
        row = jnp.concatenate(
            [
                piece.astype(BF16).reshape(-1, 128)
                for piece in (jnp.concatenate([early, late], axis=1), sums, head_sums[:, ::2])
            ]
        )
        return jnp.pad(row, ((0, -row.shape[0] % 16), (0, 0)))

    def modulation_of(shared):
        return shared[:, :vector_rows].reshape(count * latents, 6 * D)

    def ada_back(shared, silu_columns, to_owner):
        modulation_all = modulation_of(shared)
        slots = contract(modulation_all, ada_weight, 1, 1).reshape(count, latents * ada_rows)
        slots = jnp.dot(to_owner, slots, precision=lax.Precision.HIGHEST)
        return exchange(slots, axes), contract(silu_columns, modulation_all, 0, 0)

    def condition_back(slots):
        grad = slots.reshape(count, latents, ada_rows).transpose(1, 0, 2).reshape(latents, D)
        return silu_pullback(grad)[0]

    numbers = lax.broadcasted_iota(jnp.int32, (count, count), 0)
    order = lax.broadcasted_iota(jnp.int32, (count, count), 1)
    if direct:
        plane, cell = order // (count // 2), order % (count // 2)
        pair, line = cell // tensor_size, cell % tensor_size
        order = jnp.bitwise_xor(2 * pair + plane, position[0]) * tensor_size + jnp.bitwise_xor(
            line, position[1]
        )
    to_owner = (numbers == order).astype(F32)
    silu_columns = contract(
        to_owner.astype(BF16), silu_columns.reshape(count, latents * ada_rows), 0, 0
    )
    silu_columns = silu_columns.astype(BF16).reshape(count * latents, ada_rows)

    if direct:
        down_out = Flow(reduce_stages(*square_grad(mlp_grad, activated)))
        hidden_out = Flow(
            reduce_stages(*slot([down_out], (input_two, preact_grad), square_grad))
        )
        qkv_sums, carried = 0.0, ()
        for latent in range(latents):
            flows = [flow for flow in (down_out, hidden_out) if flow.value is None]
            *carried, own_sums = slot(flows, *latent_back(latent, 1, tuple(carried)))
            qkv_sums = qkv_sums + own_sums
        qkv_grad, input_grad, early_pieces = carried
        shared_in = Flow(
            vector_stages(vectors(early_pieces, late_pieces, late_sums, qkv_sums))
        )
        flows = [flow for flow in (down_out, hidden_out) if flow.value is None]
        heads_out = Flow(
            reduce_stages(
                *slot(
                    flows + [shared_in], (input_one, qkv_grad, attended_grad, mixed), heads_grad
                )
            )
        )
        slot([heads_out, shared_in], (), lambda: ())

        def finish_vectors(own, columns, order):
            both = jnp.stack([own, swap(own, across)]).reshape(count, -1, 128)
            return both, ada_back(both, columns, order)

        shared, (silu_grad, ada_weight_grad) = slot(
            [heads_out], (shared_in.value, silu_columns, to_owner), finish_vectors
        )
        condition_grad = slot([heads_out], (silu_grad,), condition_back)
        slot([heads_out], (), lambda: ())
        down_weight_grad, hidden_weight_grad = down_out.value.T, hidden_out.value
        packed_grad = heads_out.value.reshape(slab, 4, head_width)
        qkv_weight_grad = packed_grad[:, :3].swapaxes(0, 1)
        proj_weight_grad = packed_grad[:, 3].T
    else:
        inputs, run = latent_back(0, latents, ())
        qkv_grad, input_grad, early_pieces, qkv_sums = run(*inputs)
        down_weight_grad = scattered(weight_grad(mlp_grad, activated)).T
        hidden_weight_grad = scattered(weight_grad(input_two, preact_grad))
        proj_weight_grad = scattered(weight_grad(attended_grad, mixed)).T
        qkv_weight_grad = scattered(
            weight_grad(input_one, qkv_grad.reshape(-1, tokens, head_width))
        ).reshape(qkv_weight.shape)
        shared = share([vectors(early_pieces, late_pieces, late_sums, qkv_sums)], axes, count)
        silu_grad, ada_weight_grad = ada_back(shared, silu_columns, to_owner)
        condition_grad = condition_back(silu_grad)
    totals = jnp.sum(shared[:, vector_rows:].astype(F32), axis=0).reshape(-1)
    sums_end = (tensor_size + 2) * D
    rest = totals[:sums_end].reshape(tensor_size + 2, D)
    qv_bias_grad = lax.dynamic_index_in_dim(
        totals[sums_end : sums_end + 2 * D].reshape(tensor_size, 2, head_width),
        place,
        0,
        keepdims=False,
    )
    hidden_bias_grad = lax.dynamic_index_in_dim(rest, place, 0, keepdims=False)
    proj_bias_grad, down_bias_grad = rest[tensor_size], rest[tensor_size + 1]
    ada_bias_grad = lax.dynamic_index_in_dim(
        jnp.sum(modulation_of(shared).astype(F32), axis=0).reshape(count, ada_cols),
        here,
        0,
        keepdims=False,
    )
    return (
        block_out,
        input_grad,
        condition_grad,
        ada_weight_grad,
        ada_bias_grad,
        qkv_weight_grad,
        qv_bias_grad,
        proj_weight_grad,
        proj_bias_grad,
        hidden_weight_grad,
        hidden_bias_grad,
        down_weight_grad,
        down_bias_grad,
    )


def solution(mesh):
    both = ("dp", "tensor")
    placed = (
        P(both, None),
        P(both, None),
        P(both, None),
        P(both),
        P(None, "dp", "tensor"),
        P(None, "tensor"),
        P("tensor", "dp"),
        P(),
        P("dp", "tensor"),
        P("tensor"),
        P("tensor", "dp"),
        P(),
        P(both, None),
    )
    return jax.shard_map(
        functools.partial(
            on_device, dp_size=mesh.shape["dp"], tensor_size=mesh.shape["tensor"]
        ),
        mesh=mesh,
        in_specs=placed,
        out_specs=(P(both, None), P(both, None)) + placed[1:-1],
        check_vma=False,
    )
```

```python
import functools

import jax
import jax.numpy as jnp
from jax import lax
from jax.experimental import pallas as pl
from jax.experimental.pallas import tpu as pltpu
from jax.sharding import PartitionSpec as P

D = 768
HD = 64
SEQ = 256
BF16 = jnp.bfloat16
F32 = jnp.float32


def normalize_rows(values):
    centre = values - jnp.mean(values, axis=-1, keepdims=True)
    inverse = lax.rsqrt(jnp.mean(centre * centre, axis=-1, keepdims=True) + 1e-06)
    return (centre * inverse, inverse)


def norm_backward(grad_normed, normed, inverse):
    return inverse * (
        grad_normed
        - jnp.mean(grad_normed, axis=-1, keepdims=True)
        - normed * jnp.mean(grad_normed * normed, axis=-1, keepdims=True)
    )


def contract(left, right, left_axis, right_axis):
    return lax.dot_general(
        left, right, (((left_axis,), (right_axis,)), ((), ())), preferred_element_type=F32
    )


def matrix(ref, *place):
    block = ref[(slice(None),) + place]
    return block.reshape(-1, block.shape[-1])


def column_sum(values):
    return jnp.sum(values, axis=0, keepdims=True)


def head_masks(width):
    lanes = lax.broadcasted_iota(jnp.int32, (1, width), 1)
    return [
        ((lanes >= start) & (lanes < start + HD)).astype(F32).astype(BF16)
        for start in range(0, width, HD)
    ]


def head_probs(query, key):
    scores = contract(query, key, 1, 1) * HD ** (-0.5)
    raised = jnp.exp(scores - jnp.max(scores, axis=-1, keepdims=True))
    return raised * (1.0 / jnp.sum(raised, axis=-1, keepdims=True))


def attend_kernel(rows, modulation, weight, bias, input_ref, qkv_ref, mixed_ref):
    normed, _ = normalize_rows(rows[...].astype(F32))
    pieces = modulation[0]
    inputs = (normed * (1.0 + pieces[1:2]) + pieces[0:1]).astype(BF16)
    input_ref[...] = inputs
    masks = head_masks(qkv_ref.shape[-1])
    for part in range(qkv_ref.shape[0]):
        query = (contract(inputs, matrix(weight, part, 0), 1, 0) + bias[part, 0:1].astype(F32)).astype(BF16)
        key = contract(inputs, matrix(weight, part, 1), 1, 0).astype(BF16)
        value = (contract(inputs, matrix(weight, part, 2), 1, 0) + bias[part, 1:2].astype(F32)).astype(BF16)
        qkv_ref[part, 0] = query
        qkv_ref[part, 1] = key
        qkv_ref[part, 2] = value
        mixed = None
        for mask in masks:
            probs = head_probs(query * mask, key).astype(BF16)
            own = contract(probs, value * mask, 1, 0)
            mixed = own if mixed is None else mixed + own
        mixed_ref[part] = mixed.astype(BF16)


def block_kernel(
    mixed,
    rows,
    upstream_rows,
    modulation,
    proj,
    proj_bias,
    hidden,
    hidden_bias,
    down,
    down_bias,
    out_ref,
    act_ref,
    preact_grad_ref,
    mlp_grad_ref,
    input_ref,
    middle_grad_ref,
    attended_grad_ref,
    pieces_ref,
    sums_ref,
):
    parts = act_ref.shape[0]
    pieces = modulation[0]
    gate_one, shift_two, scale_two, gate_two = [pieces[k : k + 1] for k in (2, 3, 4, 5)]
    attended = proj_bias[...].astype(F32)
    for part in range(parts):
        attended = attended + contract(mixed[part], matrix(proj, part), 1, 1)
    middle = rows[...].astype(F32) + gate_one * attended
    normed, inverse = normalize_rows(middle)
    inputs = (normed * (1.0 + scale_two) + shift_two).astype(BF16)
    input_ref[...] = inputs
    upstream = upstream_rows[...].astype(F32)
    mlp_grad = (gate_two * upstream).astype(BF16)
    mlp_grad_ref[...] = mlp_grad

    @pl.when(pl.program_id(0) == 0)
    def _():
        sums_ref[...] = jnp.zeros_like(sums_ref)

    mlp = down_bias[...].astype(F32)
    input_grad = None
    root = 0.7978845608028654
    for part in range(parts):
        hidden_part = matrix(hidden, part)
        down_part = matrix(down, part)
        preact = contract(inputs, hidden_part, 1, 0) + hidden_bias[part : part + 1].astype(F32)
        square = preact * preact
        bent = jnp.tanh(root * preact * (1.0 + 0.044715 * square))
        half = 0.5 + 0.5 * bent
        activated = (preact * half).astype(BF16)
        slope = half + (0.5 * root) * preact * (1.0 - bent * bent) * (1.0 + (3 * 0.044715) * square)
        act_ref[part] = activated
        mlp = mlp + contract(activated, down_part, 1, 1)
        preact_grad = (contract(mlp_grad, down_part, 1, 0) * slope).astype(BF16)
        preact_grad_ref[part] = preact_grad
        sums_ref[part : part + 1] += column_sum(preact_grad.astype(F32))
        own = contract(preact_grad, hidden_part, 1, 1)
        input_grad = own if input_grad is None else input_grad + own
    out_ref[...] = middle + gate_two * mlp
    middle_grad = upstream + norm_backward(input_grad * (1.0 + scale_two), normed, inverse)
    middle_grad_ref[...] = middle_grad
    attended_grad = (gate_one * middle_grad).astype(BF16)
    attended_grad_ref[...] = attended_grad
    pieces_ref[0, 0:1] = column_sum(middle_grad * attended)
    pieces_ref[0, 1:2] = column_sum(input_grad)
    pieces_ref[0, 2:3] = column_sum(input_grad * normed)
    pieces_ref[0, 3:4] = column_sum(upstream * mlp)
    sums_ref[parts : parts + 1] += column_sum(attended_grad.astype(F32))
    sums_ref[parts + 1 : parts + 2] += column_sum(mlp_grad.astype(F32))


def block_settle_kernel(
    mixed,
    rows,
    upstream_rows,
    modulation,
    proj,
    proj_bias,
    hidden_own,
    hidden_other,
    hidden_bias,
    down_own,
    down_other,
    down_bias,
    place,
    *refs,
):
    made, (hidden, down) = refs[:-2], refs[-2:]

    @pl.when(pl.program_id(0) == 0)
    def _():
        for number in range(hidden.shape[1]):
            line = jnp.bitwise_xor(number, place[1])
            for pair in range(hidden_own.shape[0]):
                for core, sources in enumerate(
                    ((hidden_own, down_own), (hidden_other, down_other))
                ):
                    spot = jnp.bitwise_xor(2 * pair + core, place[0])
                    hidden[spot, line] = sources[0][pair, number]
                    down[spot, line] = sources[1][pair, number]

    block_kernel(
        mixed,
        rows,
        upstream_rows,
        modulation,
        proj,
        proj_bias,
        hidden,
        hidden_bias,
        down,
        down_bias,
        *made,
    )


def attend_back_kernel(attended_grad, qkv, proj, grad_ref, sums_ref):
    width = qkv.shape[-1]
    masks = head_masks(width)

    @pl.when(pl.program_id(0) == 0)
    def _():
        sums_ref[...] = jnp.zeros_like(sums_ref)

    for part in range(qkv.shape[0]):
        query, key, value = qkv[part, 0], qkv[part, 1], qkv[part, 2]
        mixed_grad = contract(attended_grad[...], matrix(proj, part), 1, 0).astype(BF16)
        totals = [None, None, None]
        for mask in masks:
            own_query, own_grad = query * mask, mixed_grad * mask
            probs = head_probs(own_query, key)
            probs_grad = contract(own_grad, value, 1, 1)
            scores_grad = (
                probs * (probs_grad - jnp.sum(probs * probs_grad, axis=-1, keepdims=True))
            ).astype(BF16)
            own = (
                contract(scores_grad, key * mask, 1, 0),
                contract(scores_grad, own_query, 0, 0),
                contract(probs.astype(BF16), own_grad, 0, 0),
            )
            totals = [new if old is None else old + new for old, new in zip(totals, own)]
        for kind, factor in enumerate((HD ** (-0.5), HD ** (-0.5), 1.0)):
            low = (totals[kind] * factor).astype(BF16)
            grad_ref[part, kind] = low
            sums_ref[part, kind : kind + 1] += column_sum(low.astype(F32))


def entry_back_kernel(qkv_grad, weight, rows, modulation, middle_grad, grad_ref, pieces_ref):
    input_grad = None
    for part in range(qkv_grad.shape[0]):
        for kind in range(3):
            own = contract(qkv_grad[part, kind], matrix(weight, part, kind), 1, 1)
            input_grad = own if input_grad is None else input_grad + own
    normed, inverse = normalize_rows(rows[...].astype(F32))
    pieces = modulation[0]
    grad_ref[...] = middle_grad[...] + norm_backward(
        input_grad * (1.0 + pieces[1:2]), normed, inverse
    )
    pieces_ref[0, 0:1] = column_sum(input_grad)
    pieces_ref[0, 1:2] = column_sum(input_grad * normed)


def weight_kernel(left, right, grad_ref):
    grad = contract(left[...], right[0], 0, 0)
    grad_ref[:, 0] = grad.reshape(grad_ref.shape[0], grad_ref.shape[2], -1).astype(BF16)


def whole(array, first=0):
    return pl.BlockSpec(
        array.shape, lambda step: (0,) * array.ndim, pipeline_mode=pl.Buffered(1)
    )


def row_block(array, first=0):
    lead = array.shape[:-2]
    return pl.BlockSpec(
        lead + (SEQ, array.shape[-1]), lambda step: (0,) * len(lead) + (step + first, 0)
    )


def per_latent(array, first=0):
    return pl.BlockSpec((1,) + array.shape[1:], lambda step: (step + first, 0, 0))


def scalars(array, first=0):
    return pl.BlockSpec(memory_space=pltpu.SMEM)


def kept(array, first=0):
    return pl.BlockSpec(array.shape, lambda step: (0,) * array.ndim)


def over_latents(kernel, steps, inputs, outputs, flops, first=0, carried=(), scratch=()):
    shapes = [jax.ShapeDtypeStruct(shape, kind) for _, shape, kind in outputs]
    moved = sum(a.size * a.dtype.itemsize for _, a in inputs) + sum(
        s.size * s.dtype.itemsize for s in shapes
    )
    taken = len(inputs)

    def body(*refs):
        kernel(*refs[:taken], *refs[taken + len(carried) :])

    return pl.pallas_call(
        body,
        grid=(steps,),
        in_specs=[spec(array, first) for spec, array in inputs]
        + [pl.BlockSpec(memory_space=pl.ANY) for _ in carried],
        out_specs=[spec(shape, first) for (spec, _, _), shape in zip(outputs, shapes)],
        out_shape=shapes,
        scratch_shapes=list(scratch),
        input_output_aliases={taken + number: number for number in range(len(carried))},
        cost_estimate=pl.CostEstimate(flops=flops, transcendentals=0, bytes_accessed=moved),
        compiler_params=pltpu.CompilerParams(vmem_limit_bytes=56 << 20),
    )(*[array for _, array in inputs], *carried)


class Flow:
    def __init__(self, stages):
        self.stages = stages
        self.pending = next(stages)
        self.value = None

    def advance(self, results):
        try:
            self.pending = self.stages.send(results)
        except StopIteration as end:
            self.value = end.value


def settle_heads_kernel(place, own, other, qkv_ref, proj_ref):
    flip = place[0]
    width = proj_ref.shape[-1]
    for pair in range(own.shape[0]):
        for core, source in enumerate((own, other)):
            slot = jnp.bitwise_xor(2 * pair + core, flip)
            block = source[pair, 0]
            for kind in range(3):
                qkv_ref[0, kind, slot] = block[:, kind * width : (kind + 1) * width]
            proj_ref[0, slot] = block[:, 3 * width :]


def latent_back_kernel(
    attended_grad,
    qkv,
    proj,
    weight,
    rows,
    modulation,
    middle_grad,
    heads_ref,
    grad_ref,
    pieces_ref,
    sums_ref,
):
    attend_back_kernel(attended_grad, qkv, proj, heads_ref, sums_ref)
    entry_back_kernel(heads_ref, weight, rows, modulation, middle_grad, grad_ref, pieces_ref)


def split_rows(place, grad, keep_ref, send_ref, lanes):
    slab = keep_ref.shape[2]
    core = jnp.bitwise_and(place[0], 1)
    flip = place[0] // 2
    for pair in range(keep_ref.shape[0]):
        low = grad[2 * pair * slab : (2 * pair + 1) * slab]
        high = grad[(2 * pair + 1) * slab : (2 * pair + 2) * slab]
        slot = jnp.bitwise_xor(pair, flip)
        keep_ref[slot, 0, :, lanes] = jnp.where(core == 0, low, high).astype(BF16)
        send_ref[slot, 0, :, lanes] = jnp.where(core == 0, high, low).astype(BF16)


def weight_split_kernel(place, left, right, keep_ref, send_ref):
    split_rows(place, contract(left[...], right[0], 0, 0), keep_ref, send_ref, slice(None))


def heads_split_kernel(place, entry, qkv_grad, outer, mixed, keep_ref, send_ref):
    width = mixed.shape[-1]
    for kind in range(3):
        grad = contract(entry[...], qkv_grad[0, kind], 0, 0)
        split_rows(place, grad, keep_ref, send_ref, slice(kind * width, (kind + 1) * width))
    grad = contract(outer[...], mixed[0], 0, 0)
    split_rows(place, grad, keep_ref, send_ref, slice(3 * width, 4 * width))


def placed_call(kernel, place, steps, inputs, outputs, flops):
    shapes = [jax.ShapeDtypeStruct(shape, kind) for _, shape, kind in outputs]
    moved = sum(a.size * a.dtype.itemsize for _, a in inputs) + sum(
        s.size * s.dtype.itemsize for s in shapes
    )
    return pl.pallas_call(
        kernel,
        grid_spec=pltpu.PrefetchScalarGridSpec(
            num_scalar_prefetch=1,
            grid=(steps,),
            in_specs=[spec(array) for spec, array in inputs],
            out_specs=[spec(shape) for (spec, _, _), shape in zip(outputs, shapes)],
        ),
        out_shape=shapes,
        cost_estimate=pl.CostEstimate(flops=flops, transcendentals=0, bytes_accessed=moved),
        compiler_params=pltpu.CompilerParams(vmem_limit_bytes=56 << 20),
    )(place, *[array for _, array in inputs])


def resident(array):
    return pl.BlockSpec(
        array.shape, lambda step, place: (0,) * array.ndim, pipeline_mode=pl.Buffered(1)
    )


def by_first(array):
    rest = (0,) * (array.ndim - 1)
    return pl.BlockSpec((1,) + array.shape[1:], lambda step, place: (step,) + rest)


def to_first(array):
    rest = (0,) * (array.ndim - 1)
    return pl.BlockSpec(
        (1,) + array.shape[1:], lambda step, place: (jnp.bitwise_xor(step, place[1]),) + rest
    )


def by_second(array):
    shape = array.shape
    return pl.BlockSpec((shape[0], 1) + shape[2:], lambda step, place: (0, step, 0, 0))


def to_second(array):
    shape = array.shape
    return pl.BlockSpec(
        (shape[0], 1) + shape[2:], lambda step, place: (0, jnp.bitwise_xor(step, place[1]), 0, 0)
    )


def weight_grad(left, right, groups=1):
    batch, tokens, width = right.shape
    shape = (groups, batch, D // groups, width)
    return pl.pallas_call(
        weight_kernel,
        grid=(batch,),
        in_specs=[whole(left), pl.BlockSpec((1, tokens, width), lambda step: (step, 0, 0))],
        out_specs=pl.BlockSpec(
            (groups, 1, D // groups, width), lambda step: (0, step, 0, 0)
        ),
        out_shape=jax.ShapeDtypeStruct(shape, BF16),
        cost_estimate=pl.CostEstimate(
            flops=2 * D * batch * tokens * width, transcendentals=0, bytes_accessed=4 * D * batch * width
        ),
        compiler_params=pltpu.CompilerParams(vmem_limit_bytes=56 << 20),
    )(left, right)


def exchange(slots, axes):
    count, size = slots.shape
    rows = -(-size // 128)
    padded = jnp.pad(slots, ((0, 0), (0, rows * 128 - size))).reshape(count, rows, 128)
    return lax.all_to_all(padded, axes, 0, 0, tiled=True).reshape(count, -1)[:, :size]


def share(pieces, axes, count):
    row = jnp.concatenate([piece.astype(BF16).reshape(-1, 128) for piece in pieces])
    rows = row.shape[0]
    row = jnp.pad(row, ((0, -rows % 8), (0, 0)))
    return lax.all_to_all(
        jnp.broadcast_to(row[None], (count,) + row.shape), axes, 0, 0, tiled=True
    )[:, :rows]


def on_device(
    latents_in,
    condition,
    ada_weight,
    ada_bias,
    qkv_weight,
    qv_bias,
    proj_weight,
    proj_bias,
    hidden_weight,
    hidden_bias,
    down_weight,
    down_bias,
    upstream_grad,
    dp_size,
    tensor_size,
):
    axes = ("dp", "tensor")
    count = dp_size * tensor_size
    latents = condition.shape[0]
    tokens = latents_in.shape[0]
    ada_rows, ada_cols = ada_weight.shape[0], ada_bias.shape[0]
    here = lax.axis_index("dp") * tensor_size + lax.axis_index("tensor")
    place = lax.axis_index("tensor")
    slab = D // dp_size
    direct = dp_size == 8 and tensor_size == 4 and slab % 16 == 0
    head_width, hidden_width = qkv_weight.shape[2], hidden_weight.shape[1]

    silu_value, silu_pullback = jax.vjp(jax.nn.silu, condition.astype(F32))
    silu_cond = silu_value.astype(BF16)
    def packed_slots(weight, silu_rows):
        return jnp.concatenate(
            [
                weight.reshape(ada_rows, count, ada_cols).transpose(1, 0, 2).reshape(count, -1),
                silu_rows.reshape(latents, count, ada_rows).transpose(1, 0, 2).reshape(count, -1),
                jnp.broadcast_to(
                    jnp.concatenate([silu_rows.reshape(-1), qv_bias.reshape(-1), hidden_bias])[
                        None
                    ],
                    (count, latents * D + 2 * head_width + hidden_width),
                ),
            ],
            axis=1,
        )

    def swap(array, mask):
        return lax.ppermute(array, axes, [(device, device ^ mask) for device in range(count)])

    def slot(flows, inputs, run):
        moving = [[array for array, _ in flow.pending] for flow in flows]
        moving, inputs = lax.optimization_barrier((moving, inputs))
        results = [
            [swap(array, mask) for array, (_, mask) in zip(arrays, flow.pending)]
            for arrays, flow in zip(moving, flows)
        ]
        results, made = lax.optimization_barrier((results, run(*inputs)))
        for flow, arrived in zip(flows, results):
            flow.advance(arrived)
        return made

    across, along, upward = [tensor_size << bit for bit in range(3)]
    half = tensor_size // 2
    position = jnp.stack([lax.axis_index("dp"), place])

    def gather_stages(shard):
        line = yield [(shard, mask) for mask in range(1, tensor_size)]
        line = jnp.stack([shard] + line)
        side, above = yield [(line, along), (line, upward)]
        first, second = yield [(side[:half], upward), (above[half:], along)]
        own = jnp.stack([line, side, above, jnp.concatenate([first, second])])
        (other,) = yield [(own, across)]
        return own, other

    def vector_stages(row):
        line = yield [(row, mask) for mask in range(1, tensor_size)]
        line = jnp.stack([row] + line)
        near = yield [(line, along), (line, upward), (line, along + upward)]
        return jnp.stack([line] + near)

    def reduce_stages(keep, send):
        (arrived,) = yield [(send, across)]
        summed = keep.astype(F32) + arrived.astype(F32)
        line, side, above, far = [summed[number] for number in range(4)]
        moved = [
            jnp.concatenate(pair).astype(BF16)
            for pair in ((side[:half], far[:half]), (above[half:], far[half:]))
        ]
        arrived = yield list(zip(moved, (along, upward)))
        arrived = [block.astype(F32) for block in arrived]
        side_low, far_low = arrived[0][:half], arrived[0][half:]
        above_high, far_high = arrived[1][:half], arrived[1][half:]
        arrived = yield [
            ((above[:half] + far_low).astype(BF16), upward),
            ((side[half:] + far_high).astype(BF16), along),
        ]
        low = line[:half] + side_low + arrived[0].astype(F32)
        high = line[half:] + above_high + arrived[1].astype(F32)
        pieces = [low[number] for number in range(half)] + [high[number] for number in range(half)]
        arrived = yield [(pieces[mask].astype(BF16), mask) for mask in range(1, tensor_size)]
        return sum([block.astype(F32) for block in arrived], pieces[0])

    def gathered(shard):
        whole_set = lax.all_gather(shard, axes, axis=0)
        whole_set = whole_set.reshape((dp_size, tensor_size) + shard.shape)
        rows = whole_set.ndim - 2
        whole_set = jnp.moveaxis(whole_set, 0, rows - 1)
        return whole_set.reshape((1,) + whole_set.shape[: rows - 1] + (D, shard.shape[-1]))

    def scattered(blocks):
        blocks = blocks[0].reshape(-1, dp_size, slab, blocks.shape[-1]).swapaxes(0, 1)
        flat = blocks.reshape(-1, blocks.shape[-1])
        flat = lax.psum_scatter(flat, "dp", scatter_dimension=0, tiled=True)
        return lax.psum_scatter(flat, "tensor", scatter_dimension=0, tiled=True).astype(F32)

    def settled_heads(own, other):
        qkv_set, proj_set = placed_call(
            settle_heads_kernel,
            position,
            tensor_size,
            [(by_second, own), (by_second, other)],
            [
                (to_first, (tensor_size, 3, dp_size, slab, head_width), BF16),
                (to_first, (tensor_size, dp_size, slab, head_width), BF16),
            ],
            0,
        )
        return (
            qkv_set.reshape(1, tensor_size, 3, D, head_width),
            proj_set.reshape(1, tensor_size, D, head_width),
        )

    ends = [ada_rows * ada_cols]
    for size in (ada_rows * latents, latents * D, 2 * head_width):
        ends.append(ends[-1] + size)

    def modulate(columns):
        back = lax.all_to_all(columns, axes, 0, 0, tiled=True)
        back = back.reshape(count, -1)[:, : latents * ada_cols]
        return back.reshape(count, latents, ada_cols).transpose(1, 0, 2).reshape(latents, 6, D)

    def opened(slots):
        got = exchange(slots, axes)
        columns = jnp.dot(
            got[:, ends[1] : ends[2]].reshape(count * latents, D),
            got[:, : ends[0]].reshape(D, ada_cols),
            preferred_element_type=F32,
        )
        columns = columns + ada_bias.astype(F32)
        columns = jnp.pad(
            columns.reshape(count, latents * ada_cols), ((0, 0), (0, -latents * ada_cols % 128))
        ).reshape(count, -1, 128)
        return got, modulate(columns)

    heads_in = hidden_in = down_in = None
    if direct:
        heads_in, hidden_in, down_in = [
            Flow(gather_stages(shard))
            for shard in (
                jnp.concatenate(list(qkv_weight) + [proj_weight.T], axis=1),
                hidden_weight,
                down_weight.T,
            )
        ]
    sent = slot([heads_in] if direct else [], (ada_weight, silu_cond), packed_slots)
    got, modulation = slot([heads_in, hidden_in] if direct else [], (sent,), opened)
    silu_columns = got[:, ends[0] : ends[1]].reshape(count * latents, ada_rows)
    qv_full = got[:tensor_size, ends[2] : ends[3]].reshape(tensor_size, 2, head_width)
    hidden_bias_full = got[:tensor_size, ends[3] :]
    if direct:
        slot([heads_in, hidden_in, down_in], (), lambda: ())
        slot([heads_in, hidden_in], (), lambda: ())
    else:
        qkv_full = gathered(qkv_weight)
        proj_full = gathered(proj_weight.T)
        hidden_full = gathered(hidden_weight)
        down_full = gathered(down_weight.T)

    def spread(*last):
        return (tensor_size,) + last

    unit = 2 * tokens * D * D

    def attend(first, steps):
        def run(rows, pieces, weight, bias, *kept_back):
            return over_latents(
                attend_kernel,
                steps,
                [(row_block, rows), (per_latent, pieces), (whole, weight), (whole, bias)],
                [
                    (row_block, (tokens, D), BF16),
                    (row_block, spread(3, tokens, head_width), BF16),
                    (row_block, spread(tokens, head_width), BF16),
                ],
                2 * unit * steps,
                first,
                kept_back,
            )

        return run

    def entered(rows, pieces, bias, *weights):
        weights = settled_heads(*weights)
        return attend(0, 1)(rows, pieces, weights[0], bias), weights

    if direct:
        carried, (qkv_full, proj_full) = slot(
            [down_in], (latents_in, modulation, qv_full) + heads_in.value, entered
        )
        for latent in range(1, latents):
            flows = [flow for flow in (hidden_in, down_in) if flow.value is None]
            carried = slot(
                flows,
                (latents_in, modulation, qkv_full, qv_full) + tuple(carried),
                attend(latent, 1),
            )
        while down_in.value is None:
            slot([down_in], (), lambda: ())
    else:
        carried = attend(0, latents)(latents_in, modulation, qkv_full, qv_full)
    input_one, qkv, mixed = carried
    (
        block_out,
        activated,
        preact_grad,
        mlp_grad,
        input_two,
        middle_grad,
        attended_grad,
        late_pieces,
        late_sums,
    ) = over_latents(
        block_settle_kernel if direct else block_kernel,
        latents,
        [
            (row_block, mixed),
            (row_block, latents_in),
            (row_block, upstream_grad),
            (per_latent, modulation),
            (whole, proj_full),
            (whole, proj_bias[None]),
        ]
        + [(whole, array) for array in (hidden_in.value if direct else (hidden_full,))]
        + [(whole, hidden_bias_full)]
        + [(whole, array) for array in (down_in.value if direct else (down_full,))]
        + [(whole, down_bias[None])]
        + ([(scalars, position)] if direct else []),
        [
            (row_block, (tokens, D), F32),
            (row_block, spread(tokens, hidden_width), BF16),
            (row_block, spread(tokens, hidden_width), BF16),
            (row_block, (tokens, D), BF16),
            (row_block, (tokens, D), BF16),
            (row_block, (tokens, D), F32),
            (row_block, (tokens, D), BF16),
            (per_latent, (latents, 4, D), F32),
            (kept, (tensor_size + 2, D), F32),
        ],
        18 * unit,
        scratch=[pltpu.VMEM((dp_size, tensor_size, slab, D), BF16)] * 2 if direct else (),
    )

    split_shape = (dp_size // 2, tensor_size, slab, D)
    split_out = [(to_second, split_shape, BF16), (to_second, split_shape, BF16)]

    def square_grad(left, right):
        return placed_call(
            weight_split_kernel,
            position,
            tensor_size,
            [(resident, left), (by_first, right)],
            split_out,
            4 * unit,
        )

    def heads_grad(entry, heads, outer, inner):
        return placed_call(
            heads_split_kernel,
            position,
            tensor_size,
            [(resident, entry), (by_first, heads), (resident, outer), (by_first, inner)],
            split_out,
            4 * unit,
        )

    def latent_back(first, steps, carried):
        def run(outer, heads, proj, weight, rows, pieces, middle, *kept_back):
            return over_latents(
                latent_back_kernel,
                steps,
                [
                    (row_block, outer),
                    (row_block, heads),
                    (whole, proj),
                    (whole, weight),
                    (row_block, rows),
                    (per_latent, pieces),
                    (row_block, middle),
                ],
                [
                    (row_block, spread(3, tokens, head_width), BF16),
                    (row_block, (tokens, D), F32),
                    (per_latent, (latents, 2, D), F32),
                    (kept, spread(3, head_width), F32),
                ],
                6 * unit * steps,
                first,
                kept_back,
            )

        inputs = (attended_grad, qkv, proj_full, qkv_full, latents_in, modulation, middle_grad)
        return inputs + carried, run

    vector_rows = latents * 6 * D // 128

    def vectors(early, late, sums, head_sums):
        row = jnp.concatenate(
            [
                piece.astype(BF16).reshape(-1, 128)
                for piece in (jnp.concatenate([early, late], axis=1), sums, head_sums[:, ::2])
            ]
        )
        return jnp.pad(row, ((0, -row.shape[0] % 16), (0, 0)))

    def modulation_of(shared):
        return shared[:, :vector_rows].reshape(count * latents, 6 * D)

    def ada_back(shared, silu_columns, to_owner):
        modulation_all = modulation_of(shared)
        slots = contract(modulation_all, ada_weight, 1, 1).reshape(count, latents * ada_rows)
        slots = jnp.dot(to_owner, slots, precision=lax.Precision.HIGHEST)
        return exchange(slots, axes), contract(silu_columns, modulation_all, 0, 0)

    def condition_back(slots):
        grad = slots.reshape(count, latents, ada_rows).transpose(1, 0, 2).reshape(latents, D)
        return silu_pullback(grad)[0]

    numbers = lax.broadcasted_iota(jnp.int32, (count, count), 0)
    order = lax.broadcasted_iota(jnp.int32, (count, count), 1)
    if direct:
        plane, cell = order // (count // 2), order % (count // 2)
        pair, line = cell // tensor_size, cell % tensor_size
        order = jnp.bitwise_xor(2 * pair + plane, position[0]) * tensor_size + jnp.bitwise_xor(
            line, position[1]
        )
    to_owner = (numbers == order).astype(F32)
    silu_columns = contract(
        to_owner.astype(BF16), silu_columns.reshape(count, latents * ada_rows), 0, 0
    )
    silu_columns = silu_columns.astype(BF16).reshape(count * latents, ada_rows)

    if direct:
        down_out = Flow(reduce_stages(*square_grad(mlp_grad, activated)))
        hidden_out = Flow(
            reduce_stages(*slot([down_out], (input_two, preact_grad), square_grad))
        )
        qkv_sums, carried = 0.0, ()
        for latent in range(latents):
            flows = [flow for flow in (down_out, hidden_out) if flow.value is None]
            *carried, own_sums = slot(flows, *latent_back(latent, 1, tuple(carried)))
            qkv_sums = qkv_sums + own_sums
        qkv_grad, input_grad, early_pieces = carried
        shared_in = Flow(
            vector_stages(vectors(early_pieces, late_pieces, late_sums, qkv_sums))
        )
        flows = [flow for flow in (down_out, hidden_out) if flow.value is None]
        heads_out = Flow(
            reduce_stages(
                *slot(
                    [shared_in], (input_one, qkv_grad, attended_grad, mixed), heads_grad
                )
            )
        )
        slot([heads_out, shared_in], (), lambda: ())

        def finish_vectors(own, columns, order):
            both = jnp.stack([own, swap(own, across)]).reshape(count, -1, 128)
            return both, ada_back(both, columns, order)

        shared, (silu_grad, ada_weight_grad) = slot(
            [heads_out] + flows, (shared_in.value, silu_columns, to_owner), finish_vectors
        )
        condition_grad = slot([heads_out], (silu_grad,), condition_back)
        slot([heads_out], (), lambda: ())
        down_weight_grad, hidden_weight_grad = down_out.value.T, hidden_out.value
        packed_grad = heads_out.value.reshape(slab, 4, head_width)
        qkv_weight_grad = packed_grad[:, :3].swapaxes(0, 1)
        proj_weight_grad = packed_grad[:, 3].T
    else:
        inputs, run = latent_back(0, latents, ())
        qkv_grad, input_grad, early_pieces, qkv_sums = run(*inputs)
        down_weight_grad = scattered(weight_grad(mlp_grad, activated)).T
        hidden_weight_grad = scattered(weight_grad(input_two, preact_grad))
        proj_weight_grad = scattered(weight_grad(attended_grad, mixed)).T
        qkv_weight_grad = scattered(
            weight_grad(input_one, qkv_grad.reshape(-1, tokens, head_width))
        ).reshape(qkv_weight.shape)
        shared = share([vectors(early_pieces, late_pieces, late_sums, qkv_sums)], axes, count)
        silu_grad, ada_weight_grad = ada_back(shared, silu_columns, to_owner)
        condition_grad = condition_back(silu_grad)
    totals = jnp.sum(shared[:, vector_rows:].astype(F32), axis=0).reshape(-1)
    sums_end = (tensor_size + 2) * D
    rest = totals[:sums_end].reshape(tensor_size + 2, D)
    qv_bias_grad = lax.dynamic_index_in_dim(
        totals[sums_end : sums_end + 2 * D].reshape(tensor_size, 2, head_width),
        place,
        0,
        keepdims=False,
    )
    hidden_bias_grad = lax.dynamic_index_in_dim(rest, place, 0, keepdims=False)
    proj_bias_grad, down_bias_grad = rest[tensor_size], rest[tensor_size + 1]
    ada_bias_grad = lax.dynamic_index_in_dim(
        jnp.sum(modulation_of(shared).astype(F32), axis=0).reshape(count, ada_cols),
        here,
        0,
        keepdims=False,
    )
    return (
        block_out,
        input_grad,
        condition_grad,
        ada_weight_grad,
        ada_bias_grad,
        qkv_weight_grad,
        qv_bias_grad,
        proj_weight_grad,
        proj_bias_grad,
        hidden_weight_grad,
        hidden_bias_grad,
        down_weight_grad,
        down_bias_grad,
    )


def solution(mesh):
    both = ("dp", "tensor")
    placed = (
        P(both, None),
        P(both, None),
        P(both, None),
        P(both),
        P(None, "dp", "tensor"),
        P(None, "tensor"),
        P("tensor", "dp"),
        P(),
        P("dp", "tensor"),
        P("tensor"),
        P("tensor", "dp"),
        P(),
        P(both, None),
    )
    return jax.shard_map(
        functools.partial(
            on_device, dp_size=mesh.shape["dp"], tensor_size=mesh.shape["tensor"]
        ),
        mesh=mesh,
        in_specs=placed,
        out_specs=(P(both, None), P(both, None)) + placed[1:-1],
        check_vma=False,
    )
```
